256 devices in a mesh: dp: 4 (over x), ctx: 8 (over z), tp: 8 (over y, core).
Axes of the slice: x: 4, y: 4, z: 8, core: 2. Of those that a mesh axis runs over, the one named last changes fastest.
Arguments:
- query: bfloat16 [4096, 8192], P(('dp', 'ctx'), 'tp'), may hold values from -6 to 6
- key_in: bfloat16 [4096, 8192], P(('dp', 'ctx'), 'tp'), may hold values from -6 to 6
- value_in: bfloat16 [4096, 8192], P(('dp', 'ctx'), 'tp'), may hold values from -6 to 6
- gate: bfloat16 [4096, 8192], P(('dp', 'ctx'), 'tp'), may hold values from -6 to 6
- out_grad: bfloat16 [4096, 8192], P(('dp', 'ctx')), may hold values from -6 to 6
- proj_weight: bfloat16 [8192, 8192], P('tp', ('dp', 'ctx')), may hold values from -0.0625 to 0.0625
- mr_filter: bfloat16 [512, 128], P('tp'), may hold values from -0.5 to 0.5
- lr_rate: float32 [512, 16], P('tp'), may hold values from 1.953125e-05 to 0.05
- lr_residue: float32 [512, 16], P('tp'), may hold values from -0.6 to 0.6
Outputs:
- query_grad: bfloat16 [4096, 8192], P(('dp', 'ctx'), 'tp')
- conv_grad: bfloat16 [4096, 8192], P(('dp', 'ctx'), 'tp')
- gate_grad: bfloat16 [4096, 8192], P(('dp', 'ctx'), 'tp')
- weight_grad_t: bfloat16 [8192, 8192], P(('dp', 'ctx'), 'tp')
The draws below stay inside these ranges and needn't reach their ends.
All inputs are finite; a program needn't handle non-finite values.
Results may differ from the reference program's by a relative error of at most 0.028.
Values may be sent and summed in bfloat16 or wider, within the bound.
A program may use at most 128 MiB of HBM per device.

```python
import math
import jax
import jax.numpy as jnp
from jax import lax

D = 8192
GROUP = 16
MR_TAPS = 128
ORDER = 16
TOK_DEV = 128
TOKENS = 4096
N_DP = 4
N_CTX = 8


def strengthened(values, key, source, target, shards_of, factor):
    def block_of(dim):
        return (jnp.arange(values.shape[dim]) // (values.shape[dim] // shards_of)).reshape((-1,) + (1,) * (values.ndim - 1 - dim))

    first = jax.random.permutation(key, shards_of)[block_of(target)]
    second = (block_of(target) + shards_of // 2) % shards_of
    return jnp.where((block_of(source) == first) | (block_of(source) == second), factor * values, values)


def level_of(stream_key, dims, cuts, least, high):
    def one(axis_at, blocks):
        draws = jax.random.uniform(jax.random.fold_in(jax.random.fold_in(stream_key, 6), axis_at), (blocks,), jnp.float32, least / len(cuts), high / len(cuts))
        return jnp.repeat(jnp.exp(draws), dims[axis_at] // blocks).reshape((-1,) + (1,) * (len(dims) - axis_at - 1))

    gain = one(*cuts[0])
    for cut in cuts[1:]:
        gain = gain * one(*cut)
    return gain


def noise(own_key, dims, width, limit, shards=(), dtype=jnp.bfloat16):
    gain = level_of(own_key, dims, shards, -0.22, 0.18) if shards else 1.0
    drawn = jax.random.normal(own_key, dims, jnp.float32) * width * gain
    return jnp.minimum(jnp.maximum(drawn, -limit), limit).astype(dtype)


def heavy_noise(stream_key, extent, spread, limit, pieces, heavy, dtype=jnp.bfloat16):
    values = spread * jax.random.normal(stream_key, extent, jnp.float32)
    if pieces:
        values = values * level_of(stream_key, extent, pieces, -0.22, 0.18)
    return jnp.clip(strengthened(values, jax.random.fold_in(stream_key, 3), *heavy), -limit, limit).astype(dtype)


def setup_inputs(seed: int = 0) -> dict:
    keys = jax.random.split(jax.random.key(seed), 10)
    return {
        "query": noise(keys[0], (TOKENS, D), 1.0, 6.0, ((0, 32), (1, 8))),
        "key_in": noise(keys[1], (TOKENS, D), 1.0, 6.0, ((0, 32), (1, 8))),
        "value_in": noise(keys[2], (TOKENS, D), 1.0, 6.0, ((0, 32), (1, 8))),
        "gate": noise(keys[3], (TOKENS, D), 1.0, 6.0, ((0, 32), (1, 8))),
        "out_grad": heavy_noise(keys[4], (TOKENS, D), 1.0, 6.0, ((0, 32),), (0, 1, 32, 2.75)),
        "proj_weight": noise(keys[5], (D, D), D ** -0.5, 0.0625, ((0, 8), (1, 32))),
        "mr_filter": noise(keys[6], (D // GROUP, MR_TAPS), MR_TAPS ** -0.5, 0.5, ((0, 8),)),
        "lr_rate": jnp.clip(jnp.exp(math.log(0.05) - 7.8477626 * jax.random.uniform(keys[7], (D // GROUP, ORDER), jnp.float32) ** level_of(keys[7], (D // GROUP, ORDER), ((0, 8),), -0.2, 0.2)), 1.9531249563442543e-05, 0.05),
        "lr_residue": noise(keys[8], (D // GROUP, ORDER), 0.1, 0.6, ((0, 8),), jnp.float32),
    }


HIGHEST = lax.Precision.HIGHEST


def mr_matrix(filters, row_count, taps):
    out_pos = jnp.arange(row_count)[:, None]
    in_pos = jnp.arange(row_count + taps)[None, :]
    lag_index = taps + out_pos - in_pos
    valid = (lag_index >= 0) & (lag_index < taps)
    picked = jnp.take(filters, jnp.clip(lag_index, 0, taps - 1), axis=1)
    return jnp.where(valid[None], picked, jnp.zeros_like(picked))


def lr_tables(rates, residues, row_count):
    counts = jnp.arange(row_count + 1).astype(jnp.float32)
    powers = jnp.exp(-rates[None, :, :] * counts[:, None, None])
    kernel = jnp.sum(residues[None] * powers[:row_count], axis=2)
    lag_index = jnp.arange(row_count)[:, None] - jnp.arange(row_count)[None, :]
    picked = jnp.take(kernel.T, jnp.clip(lag_index, 0, row_count - 1), axis=1)
    toeplitz = jnp.where((lag_index >= 0)[None], picked, jnp.zeros_like(picked))
    carry_coef = residues[None] * powers[1:]
    end_coef = powers[:row_count][::-1]
    start_coef = powers[:row_count]
    back_coef = residues[None] * powers[1:][::-1]
    block_decay = powers[row_count].T
    return toeplitz, carry_coef, end_coef, start_coef, back_coef, block_decay


def reference(query, key_in, value_in, gate, out_grad, proj_weight, mr_filter, lr_rate, lr_residue):
    row_count = TOK_DEV
    groups = D // GROUP
    product = (key_in.astype(jnp.float32) * value_in.astype(jnp.float32)).astype(jnp.bfloat16)
    conv_matrix = mr_matrix(mr_filter, row_count, MR_TAPS).astype(jnp.float32)
    toeplitz, carry_coef, end_coef, start_coef, back_coef, block_decay = lr_tables(lr_rate, lr_residue, row_count)
    out_delta = jnp.dot(out_grad, proj_weight.T, preferred_element_type=jnp.float32)

    def blocked(array):
        return array.reshape(N_DP, N_CTX, row_count, D)

    def forward_block(carry, inputs):
        conv_rim, state = carry
        product_blk, query_blk, gate_blk = inputs
        extended = jnp.concatenate([conv_rim, product_blk], axis=0).astype(jnp.float32)
        extended = extended.reshape(row_count + MR_TAPS, groups, GROUP)
        conv_out = jnp.einsum("gtu,ugi->tgi", conv_matrix, extended, precision=HIGHEST).reshape(row_count, D)
        mixed = (query_blk.astype(jnp.float32) * conv_out).astype(jnp.bfloat16)
        mixed_three = mixed.astype(jnp.float32).reshape(row_count, groups, GROUP)
        local_part = jnp.einsum("gtv,vgi->tgi", toeplitz, mixed_three, precision=HIGHEST)
        carried = jnp.einsum("tgn,ngi->tgi", carry_coef, state, precision=HIGHEST)
        long_out = (local_part + carried).reshape(row_count, D)
        ends = jnp.einsum("tgn,tgi->ngi", end_coef, mixed_three, precision=HIGHEST)
        new_state = block_decay[:, :, None] * state + ends
        gated = (gate_blk.astype(jnp.float32) * long_out).astype(jnp.bfloat16)
        return (product_blk[row_count - MR_TAPS:], new_state), (conv_out, long_out, gated)

    def forward_sequence(inputs):
        start = (jnp.zeros((MR_TAPS, D), jnp.bfloat16), jnp.zeros((ORDER, groups, GROUP), jnp.float32))
        final, outputs = lax.scan(forward_block, start, inputs)
        return outputs

    conv_all, long_all, gated_all = lax.map(forward_sequence, (blocked(product), blocked(query), blocked(gate)))

    def backward_block(later, inputs):
        delta_blk, gate_blk, query_blk, conv_blk, long_blk = inputs
        seed_three = (delta_blk * gate_blk.astype(jnp.float32)).reshape(row_count, groups, GROUP)
        local_back = jnp.einsum("gtv,tgi->vgi", toeplitz, seed_three, precision=HIGHEST)
        carried_back = jnp.einsum("tgn,ngi->tgi", back_coef, later, precision=HIGHEST)
        mixed_delta = (local_back + carried_back).reshape(row_count, D)
        starts = jnp.einsum("tgn,tgi->ngi", start_coef, seed_three, precision=HIGHEST)
        new_later = block_decay[:, :, None] * later + starts
        query_grad = (mixed_delta * conv_blk).astype(jnp.bfloat16)
        conv_grad = (mixed_delta * query_blk.astype(jnp.float32)).astype(jnp.bfloat16)
        gate_grad = (delta_blk * long_blk).astype(jnp.bfloat16)
        return new_later, (query_grad, conv_grad, gate_grad)

    def backward_sequence(inputs):
        start = jnp.zeros((ORDER, groups, GROUP), jnp.float32)
        final, outputs = lax.scan(backward_block, start, inputs, reverse=True)
        return outputs

    grads = lax.map(backward_sequence, (blocked(out_delta), blocked(gate), blocked(query), conv_all, long_all))
    query_grad, conv_grad, gate_grad = [item.reshape(TOKENS, D) for item in grads]

    def weight_block(total, inputs):
        delta_blk, gated_blk = inputs
        term = jnp.dot(delta_blk.T, gated_blk, preferred_element_type=jnp.float32)
        rounded = lax.optimization_barrier(term.astype(jnp.bfloat16))
        return total + rounded.astype(jnp.float32), None

    block_total = TOKENS // TOK_DEV
    weight_sum, unused = lax.scan(weight_block, jnp.zeros((D, D), jnp.float32),
                                  (out_grad.reshape(block_total, TOK_DEV, D), gated_all.reshape(block_total, TOK_DEV, D)))
    return query_grad, conv_grad, gate_grad, weight_sum.astype(jnp.bfloat16)
```

```python
import jax
import jax.numpy as jnp
from jax import lax
from jax.experimental import pallas as pl
from jax.experimental.pallas import tpu as pltpu
from jax.sharding import PartitionSpec as P

GROUP = 16
ORDER = 16
ROWS = 128
WIDTH = 1024
LANES = 128
BLOCKS = WIDTH // LANES
N_DP = 4
N_CTX = 8
N_Y = 4
FEATS = 256
HALF = WIDTH // 2

MESH = pl.DeviceIdType.MESH
HIGHEST = lax.Precision.HIGHEST
BF16 = jnp.bfloat16
F32 = jnp.float32


def remote(src, dst, send, recv, **device):
    return pltpu.make_async_remote_copy(
        src_ref=src, dst_ref=dst, send_sem=send, recv_sem=recv, device_id=device, device_id_type=MESH
    )


def iota(dim, shape=(ROWS, LANES)):
    return lax.broadcasted_iota(jnp.int32, shape, dim)


def skew(row):
    return pltpu.roll(jnp.broadcast_to(row, (ROWS, LANES)), 0, 1, stride=1, stride_axis=0)


def dot(a, b, a_dim=1, b_dim=0, precision=None):
    return lax.dot_general(
        a, b, (((a_dim,), (b_dim,)), ((), ())), precision=precision, preferred_element_type=F32
    )


def own_groups(stacked):
    lane_group = iota(1) // GROUP
    total = jnp.zeros((ROWS, LANES), F32)
    for g in range(LANES // GROUP):
        total = jnp.where(lane_group == g, stacked[g * ROWS : (g + 1) * ROWS], total)
    return total


def fold_modes(modes):
    own = jnp.where(iota(0) // ORDER == iota(1) // GROUP, modes, 0.0)
    total = own[:ORDER]
    for g in range(1, LANES // GROUP):
        total = total + own[g * ORDER : (g + 1) * ORDER]
    return total


def split(value):
    high = value.astype(BF16)
    return high, (value - high.astype(F32)).astype(BF16)


def modal(coef, state):
    spread = jnp.where(
        iota(0) // ORDER == iota(1) // GROUP, jnp.concatenate([state] * (LANES // GROUP), axis=0), 0.0
    )
    coef_high, coef_low = split(coef)
    state_high, state_low = split(spread)
    return dot(coef_high, state_high) + dot(coef_high, state_low) + dot(coef_low, state_high)


def kernel(
    q_ref, k_ref, v_ref, g_ref, og_ref, w_ref, f_ref, rate_ref, res_ref,
    qg_ref, cg_ref, gg_ref, wt_ref,
    prod, halo, og, wg, mr, tf, tb, base, coef_a, coef_e, carry, back, decay,
    conv, mixed, long_out, part, ends, ends_all, starts, starts_all, state,
    rs_out, rs_in, gall, delta, ogt, x1_out, x1_in, x2_out, x2_in,
    a2_send, a2_recv, loc, halo_sem, w_send, w_recv, y_send, y_recv, sib_send, sib_recv,
    st_send, st_recv, rs_send, rs_recv, ag_send, ag_recv, x_send, x_recv,
):
    d, c, t = lax.axis_index("dp"), lax.axis_index("ctx"), lax.axis_index("tp")
    y, core = t // 2, t % 2

    def ctx(step):
        return lax.rem(c + step + N_CTX, N_CTX)

    def dp(step):
        return lax.rem(d + step + N_DP, N_DP)

    def tp(step, side):
        return lax.rem(y + step + N_Y, N_Y) * 2 + side

    sibling = tp(0, 1 - core)

    barrier = pltpu.get_barrier_semaphore()
    for s in range(1, N_CTX):
        pl.semaphore_signal(barrier, inc=1, device_id={"ctx": ctx(s)}, device_id_type=MESH)
    for s in (-1, 1):
        pl.semaphore_signal(barrier, inc=1, device_id={"dp": dp(s)}, device_id_type=MESH)
        pl.semaphore_signal(barrier, inc=1, device_id={"tp": tp(s, core)}, device_id_type=MESH)
    pl.semaphore_signal(barrier, inc=1, device_id={"tp": sibling}, device_id_type=MESH)
    prod[...] = (k_ref[...].astype(F32) * v_ref[...].astype(F32)).astype(BF16)
    pl.semaphore_wait(barrier, N_CTX - 1 + 5)

    def strip(owner):
        return pl.ds(pl.multiple_of(owner * 16, 16), 16)

    def feature_copy(j, s):
        to = ctx(s)
        return remote(
            og_ref.at[strip(t), pl.ds(pl.multiple_of((j * N_CTX + to) * FEATS, FEATS), FEATS)],
            og.at[c, strip(t), pl.ds(j * FEATS, FEATS)],
            a2_send.at[s, j], a2_recv.at[c, j], ctx=to,
        )

    def feature_wait(j, s):
        source = ctx(s)
        remote(
            og_ref.at[strip(t), pl.ds(j * FEATS, FEATS)], og.at[source, strip(t), pl.ds(j * FEATS, FEATS)],
            a2_send.at[s, j], a2_recv.at[source, j], ctx=source,
        ).wait_recv()

    def feature_own(j):
        return pltpu.make_async_copy(
            og_ref.at[strip(t), pl.ds(pl.multiple_of((j * N_CTX + c) * FEATS, FEATS), FEATS)],
            og.at[c, strip(t), pl.ds(j * FEATS, FEATS)], loc.at[j],
        )

    for s in (4, 3, 5, 2, 6, 1, 7):
        for j in range(N_DP):
            feature_copy(j, s).start()
    halo_copy = remote(prod, halo, halo_sem.at[0], halo_sem.at[1], ctx=ctx(1))
    halo_copy.start()
    for j in range(N_DP):
        feature_own(j).start()
    w_own = pltpu.make_async_copy(w_ref, wg.at[d], loc.at[N_DP])
    w_own.start()
    steps = (1, -1)
    for way in range(2):
        remote(w_ref, wg.at[d], w_send.at[way, 0], w_recv.at[way, 0], dp=dp(steps[way])).start()

    reverse = ((iota(0) + iota(1)) % LANES == 0).astype(BF16)
    base[...] = dot(f_ref[...], reverse)
    group_of_lane = iota(1, (8, LANES)) // GROUP
    own_lane = group_of_lane == iota(0, (8, LANES))
    repeat_modes = (iota(1, (ORDER, LANES)) % ORDER == iota(0, (ORDER, LANES))).astype(F32)
    to_channels = (iota(0) // ORDER == iota(1) // GROUP).astype(F32)
    row_at = iota(0).astype(F32)

    def build(b, carried):
        rows8 = pl.ds(pl.multiple_of(b * 8, 8), 8)
        rates = jnp.where(own_lane, dot(rate_ref[rows8, :], repeat_modes, precision=HIGHEST), 0.0)
        weights = jnp.where(own_lane, dot(res_ref[rows8, :], repeat_modes, precision=HIGHEST), 0.0)
        rate = jnp.sum(rates, axis=0, keepdims=True)
        weight = jnp.sum(weights, axis=0, keepdims=True)
        falling = jnp.exp(-rate * row_at)
        rising = jnp.exp(-rate * (ROWS - 1.0 - row_at))
        once = jnp.exp(-rate)
        coef_a[b] = falling.astype(BF16)
        coef_e[b] = rising.astype(BF16)
        carry[b] = weight * once * falling
        back[b] = weight * once * rising
        per_mode = jnp.where(
            iota(1, (ORDER, LANES)) % ORDER == iota(0, (ORDER, LANES)), rate, 0.0
        )
        decay[b] = jnp.exp(-ROWS * dot(per_mode, to_channels, precision=HIGHEST))
        ahead = dot(weights, falling, b_dim=1, precision=HIGHEST)
        behind = dot(
            weights, jnp.where(iota(0) == 0, 1.0, once * rising), b_dim=1, precision=HIGHEST
        )
        taps = base[rows8, :]
        lower = iota(0) >= iota(1)
        upper = iota(1) >= iota(0)
        for g in range(8):
            here = pl.ds(g * ROWS, ROWS)
            taps_at = skew(taps[g : g + 1])
            mr[b, here, :LANES] = jnp.where(lower, taps_at, 0.0).astype(BF16)
            mr[b, here, LANES:] = jnp.where(lower, 0.0, taps_at).astype(BF16)
            tf[b, here, :] = jnp.where(lower, skew(behind[g : g + 1]), 0.0).astype(BF16)
            tb[b, here, :] = jnp.where(upper, skew(ahead[g : g + 1]), 0.0).astype(BF16)
        return carried

    lax.fori_loop(0, BLOCKS, build, 0)

    for j in range(N_DP):
        feature_own(j).wait()
        for s in range(1, N_CTX):
            feature_wait(j, s)

    def strips(owner, first=0, count=N_CTX):
        return og.at[pl.ds(first, count), strip(owner), :]

    def y_copy(owner, way, stage, first=0, count=N_CTX):
        return remote(
            strips(owner, first, count), strips(owner, first, count),
            y_send.at[way, stage], y_recv.at[way, stage], tp=tp(steps[way], core),
        )

    def sib_copy(owner, at):
        return remote(strips(owner), strips(owner), sib_send.at[at], sib_recv.at[at], tp=sibling)

    for way in range(2):
        y_copy(t, way, 0).start()
    sib_copy(t, 0).start()

    def w_relay(way):
        source = dp(-steps[way])
        rows = pl.ds(way * HALF, HALF)
        return remote(
            wg.at[source, rows, :], wg.at[source, rows, :],
            w_send.at[way, 1], w_recv.at[way, 1], dp=dp(steps[way]),
        )

    def w_relay_in(way):
        rows = pl.ds(way * HALF, HALF)
        opposite = wg.at[dp(2), rows, :]
        return remote(opposite, opposite, w_send.at[way, 1], w_recv.at[way, 1], dp=dp(steps[way]))

    halo_copy.wait_recv()

    def convolve(b, carried):
        lanes = pl.ds(pl.multiple_of(b * LANES, LANES), LANES)
        before = jnp.where(c > 0, halo[:, lanes], jnp.zeros((ROWS, LANES), BF16))
        both = jnp.concatenate([prod[:, lanes], before], axis=0)
        out = own_groups(dot(mr[b], both))
        conv[:, lanes] = out
        mix = (q_ref[:, lanes].astype(F32) * out).astype(BF16)
        mixed[:, lanes] = mix
        ends[:, lanes] = fold_modes(dot(coef_e[b], mix, a_dim=0)).astype(BF16)
        return carried

    lax.fori_loop(0, BLOCKS, convolve, 0)

    def state_copy(s):
        return remote(ends, ends_all.at[c], st_send.at[0, s], st_recv.at[0, c], ctx=ctx(s))

    for s in range(1, N_CTX):
        @pl.when(c + s < N_CTX)
        def _():
            state_copy(s).start()

    for way in range(2):
        source = dp(-steps[way])
        remote(
            w_ref, wg.at[source], w_send.at[way, 0], w_recv.at[way, 0], dp=dp(steps[way])
        ).wait_recv()
        w_relay(way).start()
    for way in range(2):
        owner = tp(-steps[way], core)
        y_copy(owner, way, 0).wait_recv()
        y_copy(owner, way, 1, way * 4, 4).start()
        sib_copy(owner, 1 + way).start()

    def local_long(b, carried):
        lanes = pl.ds(pl.multiple_of(b * LANES, LANES), LANES)
        long_out[:, lanes] = own_groups(dot(tf[b], mixed[:, lanes]))
        return carried

    lax.fori_loop(0, BLOCKS, local_long, 0)

    far = tp(2, core)
    for way in range(2):
        y_copy(far, way, 1, way * 4, 4).wait_recv()
    sib_copy(far, 3).start()

    state[...] = jnp.zeros_like(state)
    for earlier in range(N_CTX - 1):
        @pl.when(earlier < c)
        def _():
            remote(
                ends, ends_all.at[earlier], st_send.at[0, 0], st_recv.at[0, earlier], ctx=earlier
            ).wait_recv()
            for b in range(BLOCKS):
                lanes = pl.ds(b * LANES, LANES)
                state[:, lanes] = state[:, lanes] * decay[b] + ends_all[earlier, :, lanes].astype(F32)

    def finish_long(b, carried):
        lanes = pl.ds(pl.multiple_of(b * LANES, LANES), LANES)
        total = long_out[:, lanes] + modal(carry[b], state[:, lanes])
        long_out[:, lanes] = total
        gall[c, :, lanes] = (g_ref[:, lanes].astype(F32) * total).astype(BF16)
        return carried

    lax.fori_loop(0, BLOCKS, finish_long, 0)

    def ag_block(owner, half, rows):
        return gall.at[owner, rows, pl.ds(half * HALF, HALF)]

    def ag_rows(way, step):
        return pl.ds(0, ROWS) if step < 3 else pl.ds(way * 64, 64)

    def ag_copy(half, way, step):
        block = ag_block(ctx(-steps[way] * step), half, ag_rows(way, step))
        return remote(
            block, block, ag_send.at[half, way, step], ag_recv.at[half, way, step], ctx=ctx(steps[way])
        )

    def ag_in(half, way, step):
        block = ag_block(ctx(-steps[way] * (step + 1)), half, ag_rows(way, step))
        return remote(
            block, block, ag_send.at[half, way, step], ag_recv.at[half, way, step], ctx=ctx(steps[way])
        )

    for half in range(2):
        for way in range(2):
            ag_copy(half, way, 0).start()

    w_own.wait()
    for way in range(2):
        w_relay_in(way).wait_recv()
    for at, owner in enumerate(
        (sibling, tp(-1, 1 - core), tp(1, 1 - core), tp(2, 1 - core))
    ):
        sib_copy(owner, at).wait_recv()

    def project(n, carried):
        channels = pl.ds(pl.multiple_of(n * FEATS, FEATS), FEATS)
        total = jnp.zeros((N_CTX * ROWS, FEATS), F32)
        rows = og[...].reshape(N_CTX * ROWS, WIDTH)
        for j in range(N_DP):
            total = total + dot(rows[:, j * FEATS : (j + 1) * FEATS], wg[j, channels, :], b_dim=1)
        part[:, :, channels] = total.reshape(N_CTX, ROWS, FEATS)
        return carried

    lax.fori_loop(0, WIDTH // FEATS, project, 0)

    def rs_rows(way, step):
        return pl.ds(way * 64, 64) if step == 0 else pl.ds(0, ROWS)

    def rs_copy(way, step):
        rows = rs_rows(way, step)
        return remote(
            rs_out.at[way, step, rows, :], rs_in.at[way, step, rows, :],
            rs_send.at[way, step], rs_recv.at[way, step], ctx=ctx(steps[way]),
        )

    for step in range(4):
        for way in range(2):
            target = ctx(steps[way] * (4 - step))
            if step == 0:
                rows = rs_rows(way, 0)
                rs_out[way, 0, rows, :] = part[target, rows, :].astype(BF16)
            else:
                rs_copy(way, step - 1).wait_recv()
                if step == 1:
                    rows, rest = rs_rows(way, 0), rs_rows(1 - way, 0)
                    rs_out[way, 1, rows, :] = (
                        part[target, rows, :] + rs_in[way, 0, rows, :].astype(F32)
                    ).astype(BF16)
                    rs_out[way, 1, rest, :] = part[target, rest, :].astype(BF16)
                else:
                    rs_out[way, step] = (
                        part[target] + rs_in[way, step - 1].astype(F32)
                    ).astype(BF16)
            rs_copy(way, step).start()
        if step > 0:
            for half in range(2):
                for way in range(2):
                    ag_in(half, way, step - 1).wait_recv()
                    ag_copy(half, way, step).start()
        if step == 0:
            for at in range(N_CTX):
                ogt[:, at * ROWS : (at + 1) * ROWS] = og[at].T

    for way in range(2):
        rs_copy(way, 3).wait_recv()

    def seed_of(lanes):
        return delta[:, lanes] * g_ref[:, lanes].astype(F32)

    def begin_back(b, carried):
        lanes = pl.ds(pl.multiple_of(b * LANES, LANES), LANES)
        total = (
            part[c, :, lanes] + rs_in[0, 3, :, lanes].astype(F32) + rs_in[1, 3, :, lanes].astype(F32)
        )
        delta[:, lanes] = total
        gg_ref[:, lanes] = (total * long_out[:, lanes]).astype(BF16)
        seed = (total * g_ref[:, lanes].astype(F32)).astype(BF16)
        starts[:, lanes] = fold_modes(dot(coef_a[b], seed, a_dim=0)).astype(BF16)
        return carried

    lax.fori_loop(0, BLOCKS, begin_back, 0)

    def back_copy(s):
        return remote(starts, starts_all.at[c], st_send.at[1, s], st_recv.at[1, c], ctx=ctx(-s))

    for s in range(1, N_CTX):
        @pl.when(c - s >= 0)
        def _():
            back_copy(s).start()

    def weight_part(half, owner, first=0, count=FEATS):
        channels = pl.ds(half * HALF, HALF)
        rows = pl.ds(pl.multiple_of(owner * FEATS + first, 128), count)
        gated = gall[:, :, channels].reshape(N_CTX * ROWS, HALF)
        return dot(ogt[rows, :], gated)

    def x1_copy(half, way):
        return remote(
            x1_out.at[half, way], x1_in.at[half, way],
            x_send.at[half, way, 0], x_recv.at[half, way, 0], dp=dp(steps[way]),
        )

    def x2_copy(half, way):
        return remote(
            x2_out.at[half, way], x2_in.at[half, way],
            x_send.at[half, way, 1], x_recv.at[half, way, 1], dp=dp(steps[way]),
        )

    for half in range(2):
        for way in range(2):
            ag_in(half, way, 3).wait_recv()
        opposite = weight_part(half, dp(2))
        for way in range(2):
            x1_out[half, way] = opposite[way * 128 : (way + 1) * 128].astype(BF16)
            x1_copy(half, way).start()

    def local_back(b, carried):
        lanes = pl.ds(pl.multiple_of(b * LANES, LANES), LANES)
        conv_seed = seed_of(lanes).astype(BF16)
        delta[:, lanes] = own_groups(dot(tb[b], conv_seed))
        return carried

    for half in range(2):
        for way in range(2):
            near = weight_part(half, dp(steps[way]))
            x1_copy(half, way).wait_recv()
            mine, other = slice(way * 128, way * 128 + 128), slice((1 - way) * 128, (1 - way) * 128 + 128)
            x2_out[half, way, mine, :] = (near[mine] + x1_in[half, way].astype(F32)).astype(BF16)
            x2_out[half, way, other, :] = near[other].astype(BF16)
            x2_copy(half, way).start()
        if half == 0:
            lax.fori_loop(0, BLOCKS, local_back, 0)

    state[...] = jnp.zeros_like(state)
    for later in range(N_CTX - 1, 0, -1):
        @pl.when(later > c)
        def _():
            remote(
                starts, starts_all.at[later], st_send.at[1, 0], st_recv.at[1, later], ctx=later
            ).wait_recv()
            for b in range(BLOCKS):
                lanes = pl.ds(b * LANES, LANES)
                state[:, lanes] = state[:, lanes] * decay[b] + starts_all[later, :, lanes].astype(F32)

    def finish_back(b, carried):
        lanes = pl.ds(pl.multiple_of(b * LANES, LANES), LANES)
        total = delta[:, lanes] + modal(back[b], state[:, lanes])
        qg_ref[:, lanes] = (total * conv[:, lanes]).astype(BF16)
        cg_ref[:, lanes] = (total * q_ref[:, lanes].astype(F32)).astype(BF16)
        return carried

    lax.fori_loop(0, BLOCKS, finish_back, 0)

    for half in range(2):
        own = weight_part(half, d)
        for way in range(2):
            x2_copy(half, way).wait_recv()
            own = own + x2_in[half, way].astype(F32)
        wt_ref[:, half * HALF : (half + 1) * HALF] = own.astype(BF16)

    for s in range(1, N_CTX):
        for j in range(N_DP):
            feature_copy(j, s).wait_send()

        @pl.when(c + s < N_CTX)
        def _():
            state_copy(s).wait_send()

        @pl.when(c - s >= 0)
        def _():
            back_copy(s).wait_send()
    halo_copy.wait_send()
    for way in range(2):
        remote(w_ref, wg.at[d], w_send.at[way, 0], w_recv.at[way, 0], dp=dp(steps[way])).wait_send()
        w_relay(way).wait_send()
        y_copy(t, way, 0).wait_send()
        y_copy(tp(-steps[way], core), way, 1, way * 4, 4).wait_send()
        for step in range(4):
            rs_copy(way, step).wait_send()
            for half in range(2):
                ag_copy(half, way, step).wait_send()
        for half in range(2):
            x1_copy(half, way).wait_send()
            x2_copy(half, way).wait_send()
    for at, owner in enumerate((t, tp(-1, core), tp(1, core), far)):
        sib_copy(owner, at).wait_send()


def on_device(*args):
    vmem = pl.BlockSpec(memory_space=pltpu.VMEM)
    hbm = pl.BlockSpec(memory_space=pl.ANY)
    act = jax.ShapeDtypeStruct((ROWS, WIDTH), BF16)
    dma = pltpu.SemaphoreType.DMA
    stacked = (BLOCKS, 8 * ROWS, LANES)
    return pl.pallas_call(
        kernel,
        out_shape=(act, act, act, jax.ShapeDtypeStruct((FEATS, WIDTH), BF16)),
        in_specs=[vmem, vmem, vmem, vmem, hbm, hbm, vmem, vmem, vmem],
        out_specs=(vmem, vmem, vmem, vmem),
        scratch_shapes=[
            pltpu.VMEM((ROWS, WIDTH), BF16),
            pltpu.VMEM((ROWS, WIDTH), BF16),
            pltpu.VMEM((N_CTX, ROWS, WIDTH), BF16),
            pltpu.VMEM((N_DP, WIDTH, FEATS), BF16),
            pltpu.VMEM((BLOCKS, 8 * ROWS, 2 * LANES), BF16),
            pltpu.VMEM(stacked, BF16),
            pltpu.VMEM(stacked, BF16),
            pltpu.VMEM((WIDTH // GROUP, LANES), F32),
            pltpu.VMEM((BLOCKS, ROWS, LANES), BF16),
            pltpu.VMEM((BLOCKS, ROWS, LANES), BF16),
            pltpu.VMEM((BLOCKS, ROWS, LANES), F32),
            pltpu.VMEM((BLOCKS, ROWS, LANES), F32),
            pltpu.VMEM((BLOCKS, ORDER, LANES), F32),
            pltpu.VMEM((ROWS, WIDTH), F32),
            pltpu.VMEM((ROWS, WIDTH), BF16),
            pltpu.VMEM((ROWS, WIDTH), F32),
            pltpu.VMEM((N_CTX, ROWS, WIDTH), F32),
            pltpu.VMEM((ORDER, WIDTH), BF16),
            pltpu.VMEM((N_CTX, ORDER, WIDTH), BF16),
            pltpu.VMEM((ORDER, WIDTH), BF16),
            pltpu.VMEM((N_CTX, ORDER, WIDTH), BF16),
            pltpu.VMEM((ORDER, WIDTH), F32),
            pltpu.VMEM((2, 4, ROWS, WIDTH), BF16),
            pltpu.VMEM((2, 4, ROWS, WIDTH), BF16),
            pltpu.VMEM((N_CTX, ROWS, WIDTH), BF16),
            pltpu.VMEM((ROWS, WIDTH), F32),
            pltpu.VMEM((WIDTH, N_CTX * ROWS), BF16),
            pltpu.VMEM((2, 2, 128, HALF), BF16),
            pltpu.VMEM((2, 2, 128, HALF), BF16),
            pltpu.VMEM((2, 2, FEATS, HALF), BF16),
            pltpu.VMEM((2, 2, FEATS, HALF), BF16),
            dma((N_CTX, N_DP)), dma((N_CTX, N_DP)), dma((N_DP + 1,)), dma((2,)),
            dma((2, 2)), dma((2, 2)), dma((2, 2)), dma((2, 2)), dma((4,)), dma((4,)),
            dma((2, N_CTX)), dma((2, N_CTX)), dma((2, 4)), dma((2, 4)),
            dma((2, 2, 4)), dma((2, 2, 4)), dma((2, 2, 2)), dma((2, 2, 2)),
        ],
        compiler_params=pltpu.CompilerParams(
            collective_id=0, has_side_effects=True, vmem_limit_bytes=56 * 1024 * 1024
        ),
        name="hyena_backward",
    )(*args)


def solution(mesh):
    rows = P(("dp", "ctx"), "tp")
    return jax.shard_map(
        on_device,
        mesh=mesh,
        in_specs=(
            rows, rows, rows, rows, P(("dp", "ctx"), None), P("tp", ("dp", "ctx")),
            P("tp", None), P("tp", None), P("tp", None),
        ),
        out_specs=(rows, rows, rows, rows),
        check_vma=False,
    )
```

```python
import jax
import jax.numpy as jnp
from jax import lax
from jax.experimental import pallas as pl
from jax.experimental.pallas import tpu as pltpu
from jax.sharding import PartitionSpec as P

GROUP = 16
ORDER = 16
ROWS = 128
WIDTH = 1024
LANES = 128
BLOCKS = WIDTH // LANES
N_DP = 4
N_CTX = 8
N_Y = 4
FEATS = 256
HALF = WIDTH // 2
HALF_BLOCKS = BLOCKS // 2

MESH = pl.DeviceIdType.MESH
HIGHEST = lax.Precision.HIGHEST
BF16 = jnp.bfloat16
F32 = jnp.float32


def remote(src, dst, send, recv, **device):
    return pltpu.make_async_remote_copy(
        src_ref=src, dst_ref=dst, send_sem=send, recv_sem=recv, device_id=device, device_id_type=MESH
    )


def iota(dim, shape=(ROWS, LANES)):
    return lax.broadcasted_iota(jnp.int32, shape, dim)


def skew(row):
    return pltpu.roll(jnp.broadcast_to(row, (ROWS, LANES)), 0, 1, stride=1, stride_axis=0)


def dot(a, b, a_dim=1, b_dim=0, precision=None):
    return lax.dot_general(
        a, b, (((a_dim,), (b_dim,)), ((), ())), precision=precision, preferred_element_type=F32
    )


def own_groups(stacked):
    lane_group = iota(1) // GROUP
    total = jnp.zeros((ROWS, LANES), F32)
    for g in range(LANES // GROUP):
        total = jnp.where(lane_group == g, stacked[g * ROWS : (g + 1) * ROWS], total)
    return total


def fold_modes(modes):
    own = jnp.where(iota(0) // ORDER == iota(1) // GROUP, modes, 0.0)
    total = own[:ORDER]
    for g in range(1, LANES // GROUP):
        total = total + own[g * ORDER : (g + 1) * ORDER]
    return total


def split(value):
    high = value.astype(BF16)
    return high, (value - high.astype(F32)).astype(BF16)


def modal(coef, state):
    spread = jnp.where(
        iota(0) // ORDER == iota(1) // GROUP, jnp.concatenate([state] * (LANES // GROUP), axis=0), 0.0
    )
    coef_high, coef_low = split(coef)
    state_high, state_low = split(spread)
    return dot(coef_high, state_high) + dot(coef_high, state_low) + dot(coef_low, state_high)


def kernel(
    q_ref, k_ref, v_ref, g_ref, og_ref, w_ref, f_ref, rate_ref, res_ref,
    qg_ref, cg_ref, gg_ref, wt_ref,
    prod, halo, og, wg, mr, tf, tb, base, rates_all, weights_all, coef_a, coef_e, carry, back, decay,
    conv, mixed, long_out, part, ends, ends_all, starts, starts_all, state,
    rs_out, rs_in, gall, delta, ogt, x_out, x_in,
    a2_send, a2_recv, loc, halo_send, halo_recv, w_send, w_recv, y_send, y_recv, sib_send, sib_recv,
    st_send, st_recv, rs_send, rs_recv, ag_send, ag_recv, x_send, x_recv,
):
    d, c, t = lax.axis_index("dp"), lax.axis_index("ctx"), lax.axis_index("tp")
    y, core = t // 2, t % 2
    halves = [pl.ds(half * HALF, HALF) for half in range(2)]
    steps = (1, -1)

    def ctx(step):
        return lax.rem(c + step + N_CTX, N_CTX)

    def dp(step):
        return lax.rem(d + step + N_DP, N_DP)

    def tp(step, side):
        return lax.rem(y + step + N_Y, N_Y) * 2 + side

    sibling = tp(0, 1 - core)

    barrier = pltpu.get_barrier_semaphore()
    for s in range(1, N_CTX):
        pl.semaphore_signal(barrier, inc=1, device_id={"ctx": ctx(s)}, device_id_type=MESH)
    for s in range(1, N_DP):
        pl.semaphore_signal(barrier, inc=1, device_id={"dp": dp(s)}, device_id_type=MESH)
    for s in range(1, N_Y):
        pl.semaphore_signal(barrier, inc=1, device_id={"tp": tp(s, core)}, device_id_type=MESH)
    pl.semaphore_signal(barrier, inc=1, device_id={"tp": sibling}, device_id_type=MESH)
    prod[...] = (k_ref[...].astype(F32) * v_ref[...].astype(F32)).astype(BF16)
    pl.semaphore_wait(barrier, (N_CTX - 1) + (N_DP - 1) + (N_Y - 1) + 1)

    def strip(owner):
        return pl.ds(pl.multiple_of(owner * 16, 16), 16)

    def feature_copy(j, s):
        to = ctx(s)
        return remote(
            og_ref.at[strip(t), pl.ds(pl.multiple_of((j * N_CTX + to) * FEATS, FEATS), FEATS)],
            og.at[c, strip(t), pl.ds(j * FEATS, FEATS)],
            a2_send.at[s, j], a2_recv.at[c, j], ctx=to,
        )

    def feature_wait(j, s):
        source = ctx(s)
        remote(
            og_ref.at[strip(t), pl.ds(j * FEATS, FEATS)], og.at[source, strip(t), pl.ds(j * FEATS, FEATS)],
            a2_send.at[s, j], a2_recv.at[source, j], ctx=source,
        ).wait_recv()

    def feature_own(j):
        return pltpu.make_async_copy(
            og_ref.at[strip(t), pl.ds(pl.multiple_of((j * N_CTX + c) * FEATS, FEATS), FEATS)],
            og.at[c, strip(t), pl.ds(j * FEATS, FEATS)], loc.at[j],
        )

    def halo_copy(half):
        lanes = halves[half]
        return remote(prod.at[:, lanes], halo.at[:, lanes], halo_send.at[half], halo_recv.at[half], ctx=ctx(1))

    def w_copy(half, s):
        rows = halves[half]
        return remote(
            w_ref.at[rows, :], wg.at[d, rows, :], w_send.at[half, s], w_recv.at[half, s], dp=dp(s)
        )

    def w_in(half, s):
        rows = halves[half]
        return remote(
            w_ref.at[rows, :], wg.at[dp(-s), rows, :], w_send.at[half, s], w_recv.at[half, s], dp=dp(s)
        )

    halo_copy(0).start()
    for s in (4, 3, 5, 2, 6, 1, 7):
        for j in range(N_DP):
            feature_copy(j, s).start()
    halo_copy(1).start()
    for j in range(N_DP):
        feature_own(j).start()
    for half in range(2):
        for s in (2, 1, 3):
            w_copy(half, s).start()
    w_own = pltpu.make_async_copy(w_ref, wg.at[d], loc.at[N_DP])
    w_own.start()

    repeat_modes = (iota(1, (ORDER, LANES)) % ORDER == iota(0, (ORDER, LANES))).astype(F32)
    base[...] = dot(f_ref[...], ((iota(0) + iota(1)) % LANES == 0).astype(BF16))
    rates_all[...] = dot(rate_ref[...], repeat_modes, a_dim=0, precision=HIGHEST)
    weights_all[...] = dot(res_ref[...], repeat_modes, a_dim=0, precision=HIGHEST)

    def eight(b):
        return pl.ds(pl.multiple_of(b * 8, 8), 8)

    def lanes_of(b):
        return pl.ds(pl.multiple_of(b * LANES, LANES), LANES)

    def own_lane():
        return iota(1, (8, LANES)) // GROUP == iota(0, (8, LANES))

    def modes(b):
        rate = jnp.sum(jnp.where(own_lane(), rates_all[eight(b), :], 0.0), axis=0, keepdims=True)
        weights = jnp.where(own_lane(), weights_all[eight(b), :], 0.0)
        return rate, weights, jnp.sum(weights, axis=0, keepdims=True)

    def build_mr(b, carried):
        taps = base[eight(b), :]
        lower = iota(0) >= iota(1)
        for g in range(8):
            here = pl.ds(g * ROWS, ROWS)
            taps_at = skew(taps[g : g + 1])
            mr[b, here, :LANES] = jnp.where(lower, taps_at, 0.0).astype(BF16)
            mr[b, here, LANES:] = jnp.where(lower, 0.0, taps_at).astype(BF16)
        rate, _, _ = modes(b)
        coef_e[b] = jnp.exp(-rate * (ROWS - 1.0 - iota(0).astype(F32))).astype(BF16)
        return carried

    def build_forward(b, carried):
        rate, weights, weight = modes(b)
        row_at = iota(0).astype(F32)
        lag = jnp.where(iota(0) == 0, 0.0, ROWS - row_at)
        carry[b] = weight * jnp.exp(-rate * (row_at + 1.0))
        per_mode = jnp.where(iota(1, (ORDER, LANES)) % ORDER == iota(0, (ORDER, LANES)), rate, 0.0)
        to_channels = (iota(0) // ORDER == iota(1) // GROUP).astype(F32)
        decay[b] = jnp.exp(-ROWS * dot(per_mode, to_channels, precision=HIGHEST))
        behind = dot(weights, jnp.exp(-rate * lag), b_dim=1, precision=HIGHEST)
        lower = iota(0) >= iota(1)
        for g in range(8):
            tf[b, pl.ds(g * ROWS, ROWS), :] = jnp.where(lower, skew(behind[g : g + 1]), 0.0).astype(BF16)
        return carried

    def build_back(b, carried):
        rate, weights, weight = modes(b)
        row_at = iota(0).astype(F32)
        falling = jnp.exp(-rate * row_at)
        coef_a[b] = falling.astype(BF16)
        back[b] = weight * jnp.exp(-rate * (ROWS - row_at))
        ahead = dot(weights, falling, b_dim=1, precision=HIGHEST)
        upper = iota(1) >= iota(0)
        for g in range(8):
            tb[b, pl.ds(g * ROWS, ROWS), :] = jnp.where(upper, skew(ahead[g : g + 1]), 0.0).astype(BF16)
        return carried

    def each(half, function):
        lax.fori_loop(half * HALF_BLOCKS, (half + 1) * HALF_BLOCKS, function, 0)

    def convolve(b, carried):
        lanes = lanes_of(b)
        before = jnp.where(c > 0, halo[:, lanes], jnp.zeros((ROWS, LANES), BF16))
        both = jnp.concatenate([prod[:, lanes], before], axis=0)
        out = own_groups(dot(mr[b], both))
        conv[:, lanes] = out
        mix = (q_ref[:, lanes].astype(F32) * out).astype(BF16)
        mixed[:, lanes] = mix
        ends[:, lanes] = fold_modes(dot(coef_e[b], mix, a_dim=0)).astype(BF16)
        return carried

    def state_copy(half, s):
        lanes = halves[half]
        return remote(
            ends.at[:, lanes], ends_all.at[c, :, lanes], st_send.at[0, half, s], st_recv.at[0, half, c], ctx=ctx(s)
        )

    def state_in(half, source):
        lanes = halves[half]
        return remote(
            ends.at[:, lanes], ends_all.at[source, :, lanes], st_send.at[0, half, 0], st_recv.at[0, half, source],
            ctx=source,
        )

    def back_copy(half, s):
        lanes = halves[half]
        return remote(
            starts.at[:, lanes], starts_all.at[c, :, lanes], st_send.at[1, half, s], st_recv.at[1, half, c],
            ctx=ctx(-s),
        )

    def back_in(half, source):
        lanes = halves[half]
        return remote(
            starts.at[:, lanes], starts_all.at[source, :, lanes], st_send.at[1, half, 0],
            st_recv.at[1, half, source], ctx=source,
        )

    def gather_states(half, incoming, received, order, wanted):
        state[:, halves[half]] = jnp.zeros((ORDER, HALF), F32)
        for source in order:
            @pl.when(wanted(source))
            def _():
                incoming(half, source).wait_recv()
                for b in range(half * HALF_BLOCKS, (half + 1) * HALF_BLOCKS):
                    lanes = pl.ds(b * LANES, LANES)
                    state[:, lanes] = state[:, lanes] * decay[b] + received[source, :, lanes].astype(F32)

    def local_long(b, carried):
        lanes = lanes_of(b)
        long_out[:, lanes] = own_groups(dot(tf[b], mixed[:, lanes]))
        return carried

    def finish_long(b, carried):
        lanes = lanes_of(b)
        total = long_out[:, lanes] + modal(carry[b], state[:, lanes])
        long_out[:, lanes] = total
        gall[c, :, lanes] = (g_ref[:, lanes].astype(F32) * total).astype(BF16)
        return carried

    def ag_block(half, way, step, ahead):
        rows = pl.ds(0, ROWS) if step < 3 else pl.ds(way * 64, 64)
        return gall.at[ctx(-steps[way] * (step + ahead)), rows, halves[half]]

    def ag_copy(half, way, step, ahead=0):
        block = ag_block(half, way, step, ahead)
        return remote(
            block, block, ag_send.at[half, way, step], ag_recv.at[half, way, step], ctx=ctx(steps[way])
        )

    def gather(half, step):
        for way in range(2):
            if step > 0:
                ag_copy(half, way, step - 1, 1).wait_recv()
            if step < 4:
                ag_copy(half, way, step).start()

    def rs_rows(way, step):
        return pl.ds(way * 64, 64) if step == 0 else pl.ds(0, ROWS)

    def rs_copy(half, way, step):
        rows = rs_rows(way, step)
        return remote(
            rs_out.at[half, way, step, rows, :], rs_in.at[half, way, step, rows, :],
            rs_send.at[half, way, step], rs_recv.at[half, way, step], ctx=ctx(steps[way]),
        )

    def reduce(half, step):
        lanes = halves[half]
        for way in range(2):
            if step > 0:
                rs_copy(half, way, step - 1).wait_recv()
            if step == 4:
                continue
            target = ctx(steps[way] * (4 - step))
            if step < 2:
                rows, rest = rs_rows(way, 0), rs_rows(1 - way, 0)
                total = part[target, rows, lanes]
                if step == 1:
                    total = total + rs_in[half, way, 0, rows, :].astype(F32)
                    rs_out[half, way, 1, rest, :] = part[target, rest, lanes].astype(BF16)
                rs_out[half, way, step, rows, :] = total.astype(BF16)
            else:
                rs_out[half, way, step] = (
                    part[target, :, lanes] + rs_in[half, way, step - 1].astype(F32)
                ).astype(BF16)
            rs_copy(half, way, step).start()

    def project(n, carried):
        channels = pl.ds(pl.multiple_of(n * FEATS, FEATS), FEATS)
        total = jnp.zeros((N_CTX * ROWS, FEATS), F32)
        rows = og[...].reshape(N_CTX * ROWS, WIDTH)
        for j in range(N_DP):
            total = total + dot(rows[:, j * FEATS : (j + 1) * FEATS], wg[j, channels, :], b_dim=1)
        part[:, :, channels] = total.reshape(N_CTX, ROWS, FEATS)
        return carried

    def project_half(half):
        for s in range(1, N_DP):
            w_in(half, s).wait_recv()
        lax.fori_loop(half * 2, half * 2 + 2, project, 0)

    def begin_back_of(half):
        def begin_back(b, carried):
            lanes = lanes_of(b)
            inner = pl.ds(pl.multiple_of((b - half * HALF_BLOCKS) * LANES, LANES), LANES)
            total = (
                part[c, :, lanes]
                + rs_in[half, 0, 3, :, inner].astype(F32)
                + rs_in[half, 1, 3, :, inner].astype(F32)
            )
            delta[:, lanes] = total
            gg_ref[:, lanes] = (total * long_out[:, lanes]).astype(BF16)
            seed = (total * g_ref[:, lanes].astype(F32)).astype(BF16)
            starts[:, lanes] = fold_modes(dot(coef_a[b], seed, a_dim=0)).astype(BF16)
            return carried

        each(half, begin_back)
        for s in range(1, N_CTX):
            @pl.when(c - s >= 0)
            def _():
                back_copy(half, s).start()

    def local_back(b, carried):
        lanes = lanes_of(b)
        seed = (delta[:, lanes] * g_ref[:, lanes].astype(F32)).astype(BF16)
        delta[:, lanes] = own_groups(dot(tb[b], seed))
        return carried

    def finish_back(b, carried):
        lanes = lanes_of(b)
        total = delta[:, lanes] + modal(back[b], state[:, lanes])
        qg_ref[:, lanes] = (total * conv[:, lanes]).astype(BF16)
        cg_ref[:, lanes] = (total * q_ref[:, lanes].astype(F32)).astype(BF16)
        return carried

    def weight_part(half, owner):
        rows = pl.ds(pl.multiple_of(owner * FEATS, FEATS), FEATS)
        return dot(ogt[rows, :], gall[:, :, halves[half]].reshape(N_CTX * ROWS, HALF))

    def x_copy(half, s):
        return remote(
            x_out.at[half, s - 1], x_in.at[half, s - 1], x_send.at[half, s], x_recv.at[half, s], dp=dp(s)
        )

    def weight_send(half):
        for s in (2, 1, 3):
            x_out[half, s - 1] = weight_part(half, dp(s)).astype(BF16)
            x_copy(half, s).start()

    def weight_finish(half):
        own = weight_part(half, d)
        for s in range(1, N_DP):
            x_copy(half, s).wait_recv()
            own = own + x_in[half, s - 1].astype(F32)
        wt_ref[:, half * HALF : (half + 1) * HALF] = own.astype(BF16)

    def strips(owner):
        return og.at[:, strip(owner), :]

    def y_copy(owner, s):
        return remote(strips(owner), strips(owner), y_send.at[s], y_recv.at[s], tp=tp(s, core))

    def sib_copy(owner, at):
        return remote(strips(owner), strips(owner), sib_send.at[at], sib_recv.at[at], tp=sibling)

    def begin_forward(half):
        halo_copy(half).wait_recv()
        each(half, convolve)
        for s in range(1, N_CTX):
            @pl.when(c + s < N_CTX)
            def _():
                state_copy(half, s).start()

    def forward(half):
        each(half, local_long)
        gather_states(half, state_in, ends_all, range(N_CTX - 1), lambda source: source < c)
        each(half, finish_long)
        gather(half, 0)

    def begin_y():
        for j in range(N_DP):
            feature_own(j).wait()
            for s in range(1, N_CTX):
                feature_wait(j, s)
        for s in (2, 1, 3):
            y_copy(t, s).start()
        sib_copy(t, 0).start()

    def forward_y():
        for s in range(1, N_Y):
            owner = tp(-s, core)
            y_copy(owner, s).wait_recv()
            sib_copy(owner, s).start()

    def transpose_rows(at, carried):
        ogt[:, pl.ds(pl.multiple_of(at * ROWS, ROWS), ROWS)] = og[at].T
        return carried

    each(0, build_mr)
    begin_forward(0)
    each(1, build_mr)
    each(0, build_forward)
    begin_y()
    begin_forward(1)
    forward(0)
    each(1, build_forward)
    forward(1)
    gather(0, 1)
    gather(1, 1)
    forward_y()
    each(0, build_back)
    gather(0, 2)
    each(1, build_back)
    gather(1, 2)
    w_own.wait()
    for s in range(N_Y):
        sib_copy(tp(-s, 1 - core), s).wait_recv()
    project_half(0)
    reduce(0, 0)
    gather(0, 3)
    project_half(1)
    reduce(1, 0)
    gather(1, 3)
    reduce(0, 1)
    lax.fori_loop(0, N_CTX, transpose_rows, 0)
    reduce(1, 1)
    gather(0, 4)
    weight_send(0)
    reduce(0, 2)
    gather(1, 4)
    reduce(1, 2)
    weight_send(1)
    reduce(0, 3)
    reduce(1, 3)
    reduce(0, 4)
    begin_back_of(0)
    each(0, local_back)
    weight_finish(0)
    reduce(1, 4)
    begin_back_of(1)
    each(1, local_back)
    gather_states(0, back_in, starts_all, range(N_CTX - 1, 0, -1), lambda source: source > c)
    each(0, finish_back)
    weight_finish(1)
    gather_states(1, back_in, starts_all, range(N_CTX - 1, 0, -1), lambda source: source > c)
    each(1, finish_back)

    for s in range(1, N_CTX):
        for j in range(N_DP):
            feature_copy(j, s).wait_send()

        @pl.when(c + s < N_CTX)
        def _():
            for half in range(2):
                state_copy(half, s).wait_send()

        @pl.when(c - s >= 0)
        def _():
            for half in range(2):
                back_copy(half, s).wait_send()
    for s in range(1, N_Y):
        y_copy(t, s).wait_send()
    for s in range(N_Y):
        sib_copy(tp(-s, core), s).wait_send()
    for half in range(2):
        halo_copy(half).wait_send()
        for s in range(1, N_DP):
            w_copy(half, s).wait_send()
            x_copy(half, s).wait_send()
        for way in range(2):
            for step in range(4):
                rs_copy(half, way, step).wait_send()
                ag_copy(half, way, step).wait_send()


def copy_out(*refs):
    count = len(refs) // 3
    results, outs, held, sems = refs[:count], refs[count : 2 * count], refs[2 * count : -1], refs[-1]
    arrive = [pltpu.make_async_copy(results[i], held[i], sems.at[0, i]) for i in range(count)]
    leave = [pltpu.make_async_copy(held[i], outs[i], sems.at[1, i]) for i in range(count)]
    for copy in arrive:
        copy.start()
    for i in range(count):
        arrive[i].wait()
        leave[i].start()
    for copy in leave:
        copy.wait()


def on_device(query, key_in, value_in, gate, out_grad, proj_weight, mr_filter, lr_rate, lr_residue):
    vmem = pl.BlockSpec(memory_space=pltpu.VMEM)
    hbm = pl.BlockSpec(memory_space=pl.ANY)
    act = jax.ShapeDtypeStruct((ROWS, WIDTH), BF16)
    outs = (act, act, act, jax.ShapeDtypeStruct((FEATS, WIDTH), BF16))
    dma = pltpu.SemaphoreType.DMA
    stacked = (BLOCKS, 8 * ROWS, LANES)
    results = pl.pallas_call(
        kernel,
        out_shape=outs,
        in_specs=[vmem, vmem, vmem, vmem, hbm, hbm, vmem, vmem, vmem],
        out_specs=(vmem, vmem, vmem, vmem),
        scratch_shapes=[
            pltpu.VMEM((ROWS, WIDTH), BF16),
            pltpu.VMEM((ROWS, WIDTH), BF16),
            pltpu.VMEM((N_CTX, ROWS, WIDTH), BF16),
            pltpu.VMEM((N_DP, WIDTH, FEATS), BF16),
            pltpu.VMEM((BLOCKS, 8 * ROWS, 2 * LANES), BF16),
            pltpu.VMEM(stacked, BF16),
            pltpu.VMEM(stacked, BF16),
            pltpu.VMEM((WIDTH // GROUP, LANES), F32),
            pltpu.VMEM((WIDTH // GROUP, LANES), F32),
            pltpu.VMEM((WIDTH // GROUP, LANES), F32),
            pltpu.VMEM((BLOCKS, ROWS, LANES), BF16),
            pltpu.VMEM((BLOCKS, ROWS, LANES), BF16),
            pltpu.VMEM((BLOCKS, ROWS, LANES), F32),
            pltpu.VMEM((BLOCKS, ROWS, LANES), F32),
            pltpu.VMEM((BLOCKS, ORDER, LANES), F32),
            pltpu.VMEM((ROWS, WIDTH), F32),
            pltpu.VMEM((ROWS, WIDTH), BF16),
            pltpu.VMEM((ROWS, WIDTH), F32),
            pltpu.VMEM((N_CTX, ROWS, WIDTH), F32),
            pltpu.VMEM((ORDER, WIDTH), BF16),
            pltpu.VMEM((N_CTX, ORDER, WIDTH), BF16),
            pltpu.VMEM((ORDER, WIDTH), BF16),
            pltpu.VMEM((N_CTX, ORDER, WIDTH), BF16),
            pltpu.VMEM((ORDER, WIDTH), F32),
            pltpu.VMEM((2, 2, 4, ROWS, HALF), BF16),
            pltpu.VMEM((2, 2, 4, ROWS, HALF), BF16),
            pltpu.VMEM((N_CTX, ROWS, WIDTH), BF16),
            pltpu.VMEM((ROWS, WIDTH), F32),
            pltpu.VMEM((WIDTH, N_CTX * ROWS), BF16),
            pltpu.VMEM((2, N_DP - 1, FEATS, HALF), BF16),
            pltpu.VMEM((2, N_DP - 1, FEATS, HALF), BF16),
            dma((N_CTX, N_DP)), dma((N_CTX, N_DP)), dma((N_DP + 1,)), dma((2,)), dma((2,)),
            dma((2, N_DP)), dma((2, N_DP)), dma((N_Y,)), dma((N_Y,)), dma((N_Y,)), dma((N_Y,)),
            dma((2, 2, N_CTX)), dma((2, 2, N_CTX)), dma((2, 2, 4)), dma((2, 2, 4)),
            dma((2, 2, 4)), dma((2, 2, 4)), dma((2, N_DP)), dma((2, N_DP)),
        ],
        compiler_params=pltpu.CompilerParams(
            collective_id=0, has_side_effects=True, vmem_limit_bytes=56 * 1024 * 1024
        ),
        name="hyena_backward",
    )(query, key_in, value_in, gate, out_grad, proj_weight, mr_filter, lr_rate.T, lr_residue.T)
    return pl.pallas_call(
        copy_out,
        out_shape=outs,
        in_specs=[hbm] * 4,
        out_specs=(hbm,) * 4,
        scratch_shapes=[pltpu.VMEM(out.shape, out.dtype) for out in outs] + [dma((2, 4))],
        name="copy_out",
    )(*results)


def solution(mesh):
    rows = P(("dp", "ctx"), "tp")
    return jax.shard_map(
        on_device,
        mesh=mesh,
        in_specs=(
            rows, rows, rows, rows, P(("dp", "ctx"), None), P("tp", ("dp", "ctx")),
            P("tp", None), P("tp", None), P("tp", None),
        ),
        out_specs=(rows, rows, rows, rows),
        check_vma=False,
    )
```

```python
import jax
import jax.numpy as jnp
from jax import lax
from jax.experimental import pallas as pl
from jax.experimental.pallas import tpu as pltpu
from jax.sharding import PartitionSpec as P

GROUP = 16
ORDER = 16
ROWS = 128
WIDTH = 1024
LANES = 128
BLOCKS = WIDTH // LANES
N_DP = 4
N_CTX = 8
N_Y = 4
FEATS = 256
HALF = WIDTH // 2
HALF_BLOCKS = BLOCKS // 2

MESH = pl.DeviceIdType.MESH
HIGHEST = lax.Precision.HIGHEST
BF16 = jnp.bfloat16
F32 = jnp.float32


def remote(src, dst, send, recv, **device):
    return pltpu.make_async_remote_copy(
        src_ref=src, dst_ref=dst, send_sem=send, recv_sem=recv, device_id=device, device_id_type=MESH
    )


def iota(dim, shape=(ROWS, LANES)):
    return lax.broadcasted_iota(jnp.int32, shape, dim)


def skew(row):
    return pltpu.roll(jnp.broadcast_to(row, (ROWS, LANES)), 0, 1, stride=1, stride_axis=0)


def dot(a, b, a_dim=1, b_dim=0, precision=None):
    return lax.dot_general(
        a, b, (((a_dim,), (b_dim,)), ((), ())), precision=precision, preferred_element_type=F32
    )


def own_groups(stacked):
    lane_group = iota(1) // GROUP
    total = jnp.zeros((ROWS, LANES), F32)
    for g in range(LANES // GROUP):
        total = jnp.where(lane_group == g, stacked[g * ROWS : (g + 1) * ROWS], total)
    return total


def fold_modes(modes):
    own = jnp.where(iota(0) // ORDER == iota(1) // GROUP, modes, 0.0)
    total = own[:ORDER]
    for g in range(1, LANES // GROUP):
        total = total + own[g * ORDER : (g + 1) * ORDER]
    return total


def split(value):
    high = value.astype(BF16)
    return high, (value - high.astype(F32)).astype(BF16)


def modal(coef, state):
    spread = jnp.where(
        iota(0) // ORDER == iota(1) // GROUP, jnp.concatenate([state] * (LANES // GROUP), axis=0), 0.0
    )
    coef_high, coef_low = split(coef)
    state_high, state_low = split(spread)
    return dot(coef_high, state_high) + dot(coef_high, state_low) + dot(coef_low, state_high)


def kernel(
    q_ref, k_ref, v_ref, g_ref, og_ref, w_ref, f_ref, rate_ref, res_ref,
    qg_ref, cg_ref, gg_ref, wt_ref,
    prod, halo, og, wg, mr, tf, tb, base, rates_all, weights_all, coef_a, coef_e, carry, back, decay,
    conv, mixed, long_out, part, ends, ends_all, starts, starts_all, state,
    rs_out, rs_in, gall, delta, ogt, x_far_out, x_far_in, x_near_out, x_near_in, wt_sum,
    a2_send, a2_recv, loc, halo_send, halo_recv, w_send, w_recv, y_send, y_recv, sib_send, sib_recv,
    st_send, st_recv, rs_send, rs_recv, ag_send, ag_recv, x_send, x_recv,
):
    d, c, t = lax.axis_index("dp"), lax.axis_index("ctx"), lax.axis_index("tp")
    y, core = t // 2, t % 2
    halves = [pl.ds(half * HALF, HALF) for half in range(2)]
    steps = (1, -1)

    def ctx(step):
        return lax.rem(c + step + N_CTX, N_CTX)

    def dp(step):
        return lax.rem(d + step + N_DP, N_DP)

    def tp(step, side):
        return lax.rem(y + step + N_Y, N_Y) * 2 + side

    sibling = tp(0, 1 - core)

    barrier = pltpu.get_barrier_semaphore()
    for s in range(1, N_CTX):
        pl.semaphore_signal(barrier, inc=1, device_id={"ctx": ctx(s)}, device_id_type=MESH)
    for s in range(1, N_DP):
        pl.semaphore_signal(barrier, inc=1, device_id={"dp": dp(s)}, device_id_type=MESH)
    for s in range(1, N_Y):
        pl.semaphore_signal(barrier, inc=1, device_id={"tp": tp(s, core)}, device_id_type=MESH)
    pl.semaphore_signal(barrier, inc=1, device_id={"tp": sibling}, device_id_type=MESH)
    prod[...] = (k_ref[...].astype(F32) * v_ref[...].astype(F32)).astype(BF16)
    pl.semaphore_wait(barrier, (N_CTX - 1) + (N_DP - 1) + (N_Y - 1) + 1)

    def strip(owner):
        return pl.ds(pl.multiple_of(owner * 16, 16), 16)

    def feature_copy(j, s):
        to = ctx(s)
        return remote(
            og_ref.at[strip(t), pl.ds(pl.multiple_of((j * N_CTX + to) * FEATS, FEATS), FEATS)],
            og.at[c, strip(t), pl.ds(j * FEATS, FEATS)],
            a2_send.at[s, j], a2_recv.at[c, j], ctx=to,
        )

    def feature_wait(j, s):
        source = ctx(s)
        remote(
            og_ref.at[strip(t), pl.ds(j * FEATS, FEATS)], og.at[source, strip(t), pl.ds(j * FEATS, FEATS)],
            a2_send.at[s, j], a2_recv.at[source, j], ctx=source,
        ).wait_recv()

    def feature_own(j):
        return pltpu.make_async_copy(
            og_ref.at[strip(t), pl.ds(pl.multiple_of((j * N_CTX + c) * FEATS, FEATS), FEATS)],
            og.at[c, strip(t), pl.ds(j * FEATS, FEATS)], loc.at[j],
        )

    def halo_copy(half):
        lanes = halves[half]
        return remote(prod.at[:, lanes], halo.at[:, lanes], halo_send.at[half], halo_recv.at[half], ctx=ctx(1))

    def w_copy(half, s):
        rows = halves[half]
        return remote(
            w_ref.at[rows, :], wg.at[d, rows, :], w_send.at[half, s], w_recv.at[half, s], dp=dp(s)
        )

    def w_in(half, s):
        rows = halves[half]
        return remote(
            w_ref.at[rows, :], wg.at[dp(-s), rows, :], w_send.at[half, s], w_recv.at[half, s], dp=dp(s)
        )

    halo_copy(0).start()
    for s in (4, 3, 5, 2, 6, 1, 7):
        for j in range(N_DP):
            feature_copy(j, s).start()
    halo_copy(1).start()
    for j in range(N_DP):
        feature_own(j).start()
    for half in range(2):
        for s in (2, 1, 3):
            w_copy(half, s).start()
    w_own = pltpu.make_async_copy(w_ref, wg.at[d], loc.at[N_DP])
    w_own.start()

    repeat_modes = (iota(1, (ORDER, LANES)) % ORDER == iota(0, (ORDER, LANES))).astype(F32)
    base[...] = dot(f_ref[...], ((iota(0) + iota(1)) % LANES == 0).astype(BF16))
    rates_all[...] = dot(rate_ref[...], repeat_modes, a_dim=0, precision=HIGHEST)
    weights_all[...] = dot(res_ref[...], repeat_modes, a_dim=0, precision=HIGHEST)

    def eight(b):
        return pl.ds(pl.multiple_of(b * 8, 8), 8)

    def lanes_of(b):
        return pl.ds(pl.multiple_of(b * LANES, LANES), LANES)

    def own_lane():
        return iota(1, (8, LANES)) // GROUP == iota(0, (8, LANES))

    def modes(b):
        rate = jnp.sum(jnp.where(own_lane(), rates_all[eight(b), :], 0.0), axis=0, keepdims=True)
        weights = jnp.where(own_lane(), weights_all[eight(b), :], 0.0)
        return rate, weights, jnp.sum(weights, axis=0, keepdims=True)

    def build_mr(b, carried):
        taps = base[eight(b), :]
        lower = iota(0) >= iota(1)
        for g in range(8):
            here = pl.ds(g * ROWS, ROWS)
            taps_at = skew(taps[g : g + 1])
            mr[b, here, :LANES] = jnp.where(lower, taps_at, 0.0).astype(BF16)
            mr[b, here, LANES:] = jnp.where(lower, 0.0, taps_at).astype(BF16)
        rate, _, _ = modes(b)
        coef_e[b] = jnp.exp(-rate * (ROWS - 1.0 - iota(0).astype(F32))).astype(BF16)
        return carried

    def build_forward(b, carried):
        rate, weights, weight = modes(b)
        row_at = iota(0).astype(F32)
        lag = jnp.where(iota(0) == 0, 0.0, ROWS - row_at)
        carry[b] = weight * jnp.exp(-rate * (row_at + 1.0))
        per_mode = jnp.where(iota(1, (ORDER, LANES)) % ORDER == iota(0, (ORDER, LANES)), rate, 0.0)
        to_channels = (iota(0) // ORDER == iota(1) // GROUP).astype(F32)
        decay[b] = jnp.exp(-ROWS * dot(per_mode, to_channels, precision=HIGHEST))
        behind = dot(weights, jnp.exp(-rate * lag), b_dim=1, precision=HIGHEST)
        lower = iota(0) >= iota(1)
        for g in range(8):
            tf[b, pl.ds(g * ROWS, ROWS), :] = jnp.where(lower, skew(behind[g : g + 1]), 0.0).astype(BF16)
        return carried

    def build_back(b, carried):
        rate, weights, weight = modes(b)
        row_at = iota(0).astype(F32)
        falling = jnp.exp(-rate * row_at)
        coef_a[b] = falling.astype(BF16)
        back[b] = weight * jnp.exp(-rate * (ROWS - row_at))
        ahead = dot(weights, falling, b_dim=1, precision=HIGHEST)
        upper = iota(1) >= iota(0)
        for g in range(8):
            tb[b, pl.ds(g * ROWS, ROWS), :] = jnp.where(upper, skew(ahead[g : g + 1]), 0.0).astype(BF16)
        return carried

    def each(half, function):
        lax.fori_loop(half * HALF_BLOCKS, (half + 1) * HALF_BLOCKS, function, 0)

    def convolve(b, carried):
        lanes = lanes_of(b)
        before = jnp.where(c > 0, halo[:, lanes], jnp.zeros((ROWS, LANES), BF16))
        both = jnp.concatenate([prod[:, lanes], before], axis=0)
        out = own_groups(dot(mr[b], both))
        conv[:, lanes] = out
        mix = (q_ref[:, lanes].astype(F32) * out).astype(BF16)
        mixed[:, lanes] = mix
        ends[:, lanes] = fold_modes(dot(coef_e[b], mix, a_dim=0)).astype(BF16)
        return carried

    def state_copy(half, s):
        lanes = halves[half]
        return remote(
            ends.at[:, lanes], ends_all.at[c, :, lanes], st_send.at[0, half, s], st_recv.at[0, half, c], ctx=ctx(s)
        )

    def state_in(half, source):
        lanes = halves[half]
        return remote(
            ends.at[:, lanes], ends_all.at[source, :, lanes], st_send.at[0, half, 0], st_recv.at[0, half, source],
            ctx=source,
        )

    def back_copy(half, s):
        lanes = halves[half]
        return remote(
            starts.at[:, lanes], starts_all.at[c, :, lanes], st_send.at[1, half, s], st_recv.at[1, half, c],
            ctx=ctx(-s),
        )

    def back_in(half, source):
        lanes = halves[half]
        return remote(
            starts.at[:, lanes], starts_all.at[source, :, lanes], st_send.at[1, half, 0],
            st_recv.at[1, half, source], ctx=source,
        )

    def gather_states(half, incoming, received, order, wanted):
        state[:, halves[half]] = jnp.zeros((ORDER, HALF), F32)
        for source in order:
            @pl.when(wanted(source))
            def _():
                incoming(half, source).wait_recv()
                for b in range(half * HALF_BLOCKS, (half + 1) * HALF_BLOCKS):
                    lanes = pl.ds(b * LANES, LANES)
                    state[:, lanes] = state[:, lanes] * decay[b] + received[source, :, lanes].astype(F32)

    def local_long(b, carried):
        lanes = lanes_of(b)
        long_out[:, lanes] = own_groups(dot(tf[b], mixed[:, lanes]))
        return carried

    def finish_long(b, carried):
        lanes = lanes_of(b)
        total = long_out[:, lanes] + modal(carry[b], state[:, lanes])
        long_out[:, lanes] = total
        gall[c, :, lanes] = (g_ref[:, lanes].astype(F32) * total).astype(BF16)
        return carried

    def rows_of(sub):
        return pl.ds(sub * 64, 64)

    def ag_copy(half, way, step, sub, ahead=0):
        block = gall.at[ctx(-steps[way] * (step + ahead)), rows_of(sub), halves[half]]
        return remote(
            block, block, ag_send.at[half, way, step, sub], ag_recv.at[half, way, step, sub], ctx=ctx(steps[way])
        )

    def gather(half, step):
        for sub in range(2):
            for way in range(2):
                if step > 0 and (step < 4 or sub == way):
                    ag_copy(half, way, step - 1, sub, 1).wait_recv()
                if step < 3 or (step == 3 and sub == way):
                    ag_copy(half, way, step, sub).start()

    def rs_copy(half, way, step, sub):
        rows = rows_of(sub)
        return remote(
            rs_out.at[half, way, step, rows, :], rs_in.at[half, way, step, rows, :],
            rs_send.at[half, way, step, sub], rs_recv.at[half, way, step, sub], ctx=ctx(steps[way]),
        )

    def reduce(half, step):
        lanes = halves[half]
        for sub in range(2):
            rows = rows_of(sub)
            for way in range(2):
                arrives = step > 1 or (step == 1 and sub == way)
                if arrives:
                    rs_copy(half, way, step - 1, sub).wait_recv()
                if step == 4 or (step == 0 and sub != way):
                    continue
                total = part[ctx(steps[way] * (4 - step)), rows, lanes]
                if arrives:
                    total = total + rs_in[half, way, step - 1, rows, :].astype(F32)
                rs_out[half, way, step, rows, :] = total.astype(BF16)
                rs_copy(half, way, step, sub).start()

    def project(n, carried):
        channels = pl.ds(pl.multiple_of(n * FEATS, FEATS), FEATS)
        total = jnp.zeros((N_CTX * ROWS, FEATS), F32)
        rows = og[...].reshape(N_CTX * ROWS, WIDTH)
        for j in range(N_DP):
            total = total + dot(rows[:, j * FEATS : (j + 1) * FEATS], wg[j, channels, :], b_dim=1)
        part[:, :, channels] = total.reshape(N_CTX, ROWS, FEATS)
        return carried

    def project_half(half):
        for s in range(1, N_DP):
            w_in(half, s).wait_recv()
        lax.fori_loop(half * 2, half * 2 + 2, project, 0)

    def begin_back_of(half):
        def begin_back(b, carried):
            lanes = lanes_of(b)
            inner = pl.ds(pl.multiple_of((b - half * HALF_BLOCKS) * LANES, LANES), LANES)
            total = (
                part[c, :, lanes]
                + rs_in[half, 0, 3, :, inner].astype(F32)
                + rs_in[half, 1, 3, :, inner].astype(F32)
            )
            delta[:, lanes] = total
            gg_ref[:, lanes] = (total * long_out[:, lanes]).astype(BF16)
            seed = (total * g_ref[:, lanes].astype(F32)).astype(BF16)
            starts[:, lanes] = fold_modes(dot(coef_a[b], seed, a_dim=0)).astype(BF16)
            return carried

        each(half, begin_back)
        for s in range(1, N_CTX):
            @pl.when(c - s >= 0)
            def _():
                back_copy(half, s).start()

    def local_back(b, carried):
        lanes = lanes_of(b)
        seed = (delta[:, lanes] * g_ref[:, lanes].astype(F32)).astype(BF16)
        delta[:, lanes] = own_groups(dot(tb[b], seed))
        return carried

    def finish_back(b, carried):
        lanes = lanes_of(b)
        total = delta[:, lanes] + modal(back[b], state[:, lanes])
        qg_ref[:, lanes] = (total * conv[:, lanes]).astype(BF16)
        cg_ref[:, lanes] = (total * q_ref[:, lanes].astype(F32)).astype(BF16)
        return carried

    def weight_part(half, owner):
        rows = pl.ds(pl.multiple_of(owner * FEATS, FEATS), FEATS)
        return dot(ogt[rows, :], gall[:, :, halves[half]].reshape(N_CTX * ROWS, HALF))

    def x_far_copy(half, way):
        return remote(
            x_far_out.at[half, way], x_far_in.at[half, way],
            x_send.at[half, way], x_recv.at[half, way], dp=dp(steps[way]),
        )

    def x_near_copy(half, way):
        return remote(
            x_near_out.at[half, way], x_near_in.at[half, way],
            x_send.at[half, 2 + way], x_recv.at[half, 2 + way], dp=dp(steps[way]),
        )

    def weight_far(half):
        opposite = weight_part(half, dp(2))
        for way in range(2):
            x_far_out[half, way] = opposite[way * 128 : (way + 1) * 128].astype(BF16)
            x_far_copy(half, way).start()

    def weight_near(half):
        for way in range(2):
            near = weight_part(half, dp(steps[way]))
            mine = slice(way * 128, way * 128 + 128)
            other = slice((1 - way) * 128, (1 - way) * 128 + 128)
            x_near_out[half, way, other, :] = near[other].astype(BF16)
            x_far_copy(half, way).wait_recv()
            x_near_out[half, way, mine, :] = (near[mine] + x_far_in[half, way].astype(F32)).astype(BF16)
            x_near_copy(half, way).start()

    def weight_own(half):
        wt_sum[half] = weight_part(half, d)

    def weight_finish(half):
        own = wt_sum[half]
        for way in range(2):
            x_near_copy(half, way).wait_recv()
            own = own + x_near_in[half, way].astype(F32)
        wt_ref[:, half * HALF : (half + 1) * HALF] = own.astype(BF16)

    def strips(owner):
        return og.at[:, strip(owner), :]

    def y_copy(owner, s):
        return remote(strips(owner), strips(owner), y_send.at[s], y_recv.at[s], tp=tp(s, core))

    def sib_copy(owner, at):
        return remote(strips(owner), strips(owner), sib_send.at[at], sib_recv.at[at], tp=sibling)

    def begin_forward(half):
        halo_copy(half).wait_recv()
        each(half, convolve)
        for s in range(1, N_CTX):
            @pl.when(c + s < N_CTX)
            def _():
                state_copy(half, s).start()

    def forward(half):
        each(half, local_long)
        gather_states(half, state_in, ends_all, range(N_CTX - 1), lambda source: source < c)
        each(half, finish_long)
        gather(half, 0)

    def begin_y():
        for j in range(N_DP):
            feature_own(j).wait()
            for s in range(1, N_CTX):
                feature_wait(j, s)
        for s in (2, 1, 3):
            y_copy(t, s).start()
        sib_copy(t, 0).start()

    def forward_y():
        for s in range(1, N_Y):
            owner = tp(-s, core)
            y_copy(owner, s).wait_recv()
            sib_copy(owner, s).start()

    def transpose_rows(at, carried):
        ogt[:, pl.ds(pl.multiple_of(at * ROWS, ROWS), ROWS)] = og[at].T
        return carried

    each(0, build_mr)
    begin_forward(0)
    each(1, build_mr)
    each(0, build_forward)
    begin_y()
    begin_forward(1)
    forward(0)
    each(1, build_forward)
    forward(1)
    gather(0, 1)
    gather(1, 1)
    forward_y()
    each(0, build_back)
    gather(0, 2)
    each(1, build_back)
    gather(1, 2)
    w_own.wait()
    for s in range(N_Y):
        sib_copy(tp(-s, 1 - core), s).wait_recv()
    project_half(0)
    reduce(0, 0)
    gather(0, 3)
    project_half(1)
    reduce(1, 0)
    gather(1, 3)
    reduce(0, 1)
    lax.fori_loop(0, N_CTX, transpose_rows, 0)
    reduce(1, 1)
    gather(0, 4)
    weight_far(0)
    reduce(0, 2)
    gather(1, 4)
    reduce(1, 2)
    weight_far(1)
    weight_near(0)
    reduce(0, 3)
    reduce(1, 3)
    reduce(0, 4)
    begin_back_of(0)
    weight_near(1)
    each(0, local_back)
    reduce(1, 4)
    begin_back_of(1)
    each(1, local_back)
    gather_states(0, back_in, starts_all, range(N_CTX - 1, 0, -1), lambda source: source > c)
    each(0, finish_back)
    weight_own(0)
    weight_own(1)
    weight_finish(0)
    gather_states(1, back_in, starts_all, range(N_CTX - 1, 0, -1), lambda source: source > c)
    each(1, finish_back)
    weight_finish(1)

    for s in range(1, N_CTX):
        for j in range(N_DP):
            feature_copy(j, s).wait_send()

        @pl.when(c + s < N_CTX)
        def _():
            for half in range(2):
                state_copy(half, s).wait_send()

        @pl.when(c - s >= 0)
        def _():
            for half in range(2):
                back_copy(half, s).wait_send()
    for s in range(1, N_Y):
        y_copy(t, s).wait_send()
    for s in range(N_Y):
        sib_copy(tp(-s, core), s).wait_send()
    for half in range(2):
        halo_copy(half).wait_send()
        for s in range(1, N_DP):
            w_copy(half, s).wait_send()
        for way in range(2):
            x_far_copy(half, way).wait_send()
            x_near_copy(half, way).wait_send()
            for step in range(4):
                for sub in range(2):
                    if step > 0 or sub == way:
                        rs_copy(half, way, step, sub).wait_send()
                    if step < 3 or sub == way:
                        ag_copy(half, way, step, sub).wait_send()


def copy_out(*refs):
    count = len(refs) // 3
    results, outs, held, sems = refs[:count], refs[count : 2 * count], refs[2 * count : -1], refs[-1]
    arrive = [pltpu.make_async_copy(results[i], held[i], sems.at[0, i]) for i in range(count)]
    leave = [pltpu.make_async_copy(held[i], outs[i], sems.at[1, i]) for i in range(count)]
    for copy in arrive:
        copy.start()
    for i in range(count):
        arrive[i].wait()
        leave[i].start()
    for copy in leave:
        copy.wait()


def on_device(query, key_in, value_in, gate, out_grad, proj_weight, mr_filter, lr_rate, lr_residue):
    vmem = pl.BlockSpec(memory_space=pltpu.VMEM)
    hbm = pl.BlockSpec(memory_space=pl.ANY)
    act = jax.ShapeDtypeStruct((ROWS, WIDTH), BF16)
    outs = (act, act, act, jax.ShapeDtypeStruct((FEATS, WIDTH), BF16))
    dma = pltpu.SemaphoreType.DMA
    stacked = (BLOCKS, 8 * ROWS, LANES)
    results = pl.pallas_call(
        kernel,
        out_shape=outs,
        in_specs=[vmem, vmem, vmem, vmem, hbm, hbm, vmem, vmem, vmem],
        out_specs=(vmem, vmem, vmem, vmem),
        scratch_shapes=[
            pltpu.VMEM((ROWS, WIDTH), BF16),
            pltpu.VMEM((ROWS, WIDTH), BF16),
            pltpu.VMEM((N_CTX, ROWS, WIDTH), BF16),
            pltpu.VMEM((N_DP, WIDTH, FEATS), BF16),
            pltpu.VMEM((BLOCKS, 8 * ROWS, 2 * LANES), BF16),
            pltpu.VMEM(stacked, BF16),
            pltpu.VMEM(stacked, BF16),
            pltpu.VMEM((WIDTH // GROUP, LANES), F32),
            pltpu.VMEM((WIDTH // GROUP, LANES), F32),
            pltpu.VMEM((WIDTH // GROUP, LANES), F32),
            pltpu.VMEM((BLOCKS, ROWS, LANES), BF16),
            pltpu.VMEM((BLOCKS, ROWS, LANES), BF16),
            pltpu.VMEM((BLOCKS, ROWS, LANES), F32),
            pltpu.VMEM((BLOCKS, ROWS, LANES), F32),
            pltpu.VMEM((BLOCKS, ORDER, LANES), F32),
            pltpu.VMEM((ROWS, WIDTH), F32),
            pltpu.VMEM((ROWS, WIDTH), BF16),
            pltpu.VMEM((ROWS, WIDTH), F32),
            pltpu.VMEM((N_CTX, ROWS, WIDTH), F32),
            pltpu.VMEM((ORDER, WIDTH), BF16),
            pltpu.VMEM((N_CTX, ORDER, WIDTH), BF16),
            pltpu.VMEM((ORDER, WIDTH), BF16),
            pltpu.VMEM((N_CTX, ORDER, WIDTH), BF16),
            pltpu.VMEM((ORDER, WIDTH), F32),
            pltpu.VMEM((2, 2, 4, ROWS, HALF), BF16),
            pltpu.VMEM((2, 2, 4, ROWS, HALF), BF16),
            pltpu.VMEM((N_CTX, ROWS, WIDTH), BF16),
            pltpu.VMEM((ROWS, WIDTH), F32),
            pltpu.VMEM((WIDTH, N_CTX * ROWS), BF16),
            pltpu.VMEM((2, 2, 128, HALF), BF16),
            pltpu.VMEM((2, 2, 128, HALF), BF16),
            pltpu.VMEM((2, 2, FEATS, HALF), BF16),
            pltpu.VMEM((2, 2, FEATS, HALF), BF16),
            pltpu.VMEM((2, FEATS, HALF), F32),
            dma((N_CTX, N_DP)), dma((N_CTX, N_DP)), dma((N_DP + 1,)), dma((2,)), dma((2,)),
            dma((2, N_DP)), dma((2, N_DP)), dma((N_Y,)), dma((N_Y,)), dma((N_Y,)), dma((N_Y,)),
            dma((2, 2, N_CTX)), dma((2, 2, N_CTX)), dma((2, 2, 4, 2)), dma((2, 2, 4, 2)),
            dma((2, 2, 4, 2)), dma((2, 2, 4, 2)), dma((2, N_DP)), dma((2, N_DP)),
        ],
        compiler_params=pltpu.CompilerParams(
            collective_id=0, has_side_effects=True, vmem_limit_bytes=56 * 1024 * 1024
        ),
        name="hyena_backward",
    )(query, key_in, value_in, gate, out_grad, proj_weight, mr_filter, lr_rate.T, lr_residue.T)
    return pl.pallas_call(
        copy_out,
        out_shape=outs,
        in_specs=[hbm] * 4,
        out_specs=(hbm,) * 4,
        scratch_shapes=[pltpu.VMEM(out.shape, out.dtype) for out in outs] + [dma((2, 4))],
        name="copy_out",
    )(*results)


def solution(mesh):
    rows = P(("dp", "ctx"), "tp")
    return jax.shard_map(
        on_device,
        mesh=mesh,
        in_specs=(
            rows, rows, rows, rows, P(("dp", "ctx"), None), P("tp", ("dp", "ctx")),
            P("tp", None), P("tp", None), P("tp", None),
        ),
        out_specs=(rows, rows, rows, rows),
        check_vma=False,
    )
```

```python
import jax
import jax.numpy as jnp
from jax import lax
from jax.experimental import pallas as pl
from jax.experimental.pallas import tpu as pltpu
from jax.sharding import PartitionSpec as P

GROUP = 16
ORDER = 16
ROWS = 128
WIDTH = 1024
LANES = 128
BLOCKS = WIDTH // LANES
N_DP = 4
N_CTX = 8
N_Y = 4
FEATS = 256
HALF = WIDTH // 2
HALF_BLOCKS = BLOCKS // 2

MESH = pl.DeviceIdType.MESH
HIGHEST = lax.Precision.HIGHEST
BF16 = jnp.bfloat16
F32 = jnp.float32


def remote(src, dst, send, recv, **device):
    return pltpu.make_async_remote_copy(
        src_ref=src, dst_ref=dst, send_sem=send, recv_sem=recv, device_id=device, device_id_type=MESH
    )


def iota(dim, shape=(ROWS, LANES)):
    return lax.broadcasted_iota(jnp.int32, shape, dim)


def skew(row):
    return pltpu.roll(jnp.broadcast_to(row, (ROWS, LANES)), 0, 1, stride=1, stride_axis=0)


def dot(a, b, a_dim=1, b_dim=0, precision=None):
    return lax.dot_general(
        a, b, (((a_dim,), (b_dim,)), ((), ())), precision=precision, preferred_element_type=F32
    )


def own_groups(stacked):
    lane_group = iota(1) // GROUP
    total = jnp.zeros((ROWS, LANES), F32)
    for g in range(LANES // GROUP):
        total = jnp.where(lane_group == g, stacked[g * ROWS : (g + 1) * ROWS], total)
    return total


def fold_modes(modes):
    own = jnp.where(iota(0) // ORDER == iota(1) // GROUP, modes, 0.0)
    total = own[:ORDER]
    for g in range(1, LANES // GROUP):
        total = total + own[g * ORDER : (g + 1) * ORDER]
    return total


def split(value):
    high = value.astype(BF16)
    return high, (value - high.astype(F32)).astype(BF16)


def modal(coef, state):
    spread = jnp.where(
        iota(0) // ORDER == iota(1) // GROUP, jnp.concatenate([state] * (LANES // GROUP), axis=0), 0.0
    )
    coef_high, coef_low = split(coef)
    state_high, state_low = split(spread)
    return dot(coef_high, state_high) + dot(coef_high, state_low) + dot(coef_low, state_high)


def kernel(
    q_ref, k_ref, v_ref, g_ref, og_ref, w_ref, f_ref, rate_ref, res_ref,
    qg_ref, cg_ref, gg_ref, wt_ref,
    prod, halo, og, wg, mr, tf, tb, base, rates_all, weights_all, coef_a, coef_e, carry, back, decay,
    conv, mixed, long_out, part, ends, ends_all, starts, starts_all, state,
    rs_out, rs_in, gall, delta, ogt, x_far_out, x_far_in, x_near_out, x_near_in, wt_sum,
    a2_send, a2_recv, loc, halo_send, halo_recv, w_send, w_recv, y_send, y_recv, sib_send, sib_recv,
    st_send, st_recv, rs_send, rs_recv, ag_send, ag_recv, x_send, x_recv,
):
    d, c, t = lax.axis_index("dp"), lax.axis_index("ctx"), lax.axis_index("tp")
    y, core = t // 2, t % 2
    halves = [pl.ds(half * HALF, HALF) for half in range(2)]
    steps = (1, -1)

    def ctx(step):
        return lax.rem(c + step + N_CTX, N_CTX)

    def dp(step):
        return lax.rem(d + step + N_DP, N_DP)

    def tp(step, side):
        return lax.rem(y + step + N_Y, N_Y) * 2 + side

    sibling = tp(0, 1 - core)

    barrier = pltpu.get_barrier_semaphore()
    for s in range(1, N_CTX):
        pl.semaphore_signal(barrier, inc=1, device_id={"ctx": ctx(s)}, device_id_type=MESH)
    for s in range(1, N_DP):
        pl.semaphore_signal(barrier, inc=1, device_id={"dp": dp(s)}, device_id_type=MESH)
    for s in range(1, N_Y):
        pl.semaphore_signal(barrier, inc=1, device_id={"tp": tp(s, core)}, device_id_type=MESH)
    pl.semaphore_signal(barrier, inc=1, device_id={"tp": sibling}, device_id_type=MESH)
    prod[...] = (k_ref[...].astype(F32) * v_ref[...].astype(F32)).astype(BF16)
    pl.semaphore_wait(barrier, (N_CTX - 1) + (N_DP - 1) + (N_Y - 1) + 1)

    def strip(owner):
        return pl.ds(pl.multiple_of(owner * 16, 16), 16)

    def feature_copy(j, s):
        to = ctx(s)
        return remote(
            og_ref.at[strip(t), pl.ds(pl.multiple_of((j * N_CTX + to) * FEATS, FEATS), FEATS)],
            og.at[c, strip(t), pl.ds(j * FEATS, FEATS)],
            a2_send.at[s, j], a2_recv.at[c, j], ctx=to,
        )

    def feature_wait(j, s):
        source = ctx(s)
        remote(
            og_ref.at[strip(t), pl.ds(j * FEATS, FEATS)], og.at[source, strip(t), pl.ds(j * FEATS, FEATS)],
            a2_send.at[s, j], a2_recv.at[source, j], ctx=source,
        ).wait_recv()

    def feature_own(j):
        return pltpu.make_async_copy(
            og_ref.at[strip(t), pl.ds(pl.multiple_of((j * N_CTX + c) * FEATS, FEATS), FEATS)],
            og.at[c, strip(t), pl.ds(j * FEATS, FEATS)], loc.at[j],
        )

    def halo_copy(half):
        lanes = halves[half]
        return remote(prod.at[:, lanes], halo.at[:, lanes], halo_send.at[half], halo_recv.at[half], ctx=ctx(1))

    def w_copy(half, s):
        rows = halves[half]
        return remote(
            w_ref.at[rows, :], wg.at[d, rows, :], w_send.at[half, s], w_recv.at[half, s], dp=dp(s)
        )

    def w_in(half, s):
        rows = halves[half]
        return remote(
            w_ref.at[rows, :], wg.at[dp(-s), rows, :], w_send.at[half, s], w_recv.at[half, s], dp=dp(s)
        )

    halo_copy(0).start()
    for s in (4, 3, 5, 2, 6, 1, 7):
        for j in range(N_DP):
            feature_copy(j, s).start()
    halo_copy(1).start()
    for j in range(N_DP):
        feature_own(j).start()
    for half in range(2):
        for s in (2, 1, 3):
            w_copy(half, s).start()
    w_own = pltpu.make_async_copy(w_ref, wg.at[d], loc.at[N_DP])
    w_own.start()

    repeat_modes = (iota(1, (ORDER, LANES)) % ORDER == iota(0, (ORDER, LANES))).astype(F32)
    base[...] = dot(f_ref[...], ((iota(0) + iota(1)) % LANES == 0).astype(BF16))
    rates_all[...] = dot(rate_ref[...], repeat_modes, a_dim=0, precision=HIGHEST)
    weights_all[...] = dot(res_ref[...], repeat_modes, a_dim=0, precision=HIGHEST)

    def eight(b):
        return pl.ds(pl.multiple_of(b * 8, 8), 8)

    def lanes_of(b):
        return pl.ds(pl.multiple_of(b * LANES, LANES), LANES)

    def own_lane():
        return iota(1, (8, LANES)) // GROUP == iota(0, (8, LANES))

    def modes(b):
        rate = jnp.sum(jnp.where(own_lane(), rates_all[eight(b), :], 0.0), axis=0, keepdims=True)
        weights = jnp.where(own_lane(), weights_all[eight(b), :], 0.0)
        return rate, weights, jnp.sum(weights, axis=0, keepdims=True)

    def build_mr(b, carried):
        taps = base[eight(b), :]
        lower = iota(0) >= iota(1)
        for g in range(8):
            here = pl.ds(g * ROWS, ROWS)
            taps_at = skew(taps[g : g + 1])
            mr[b, here, :LANES] = jnp.where(lower, taps_at, 0.0).astype(BF16)
            mr[b, here, LANES:] = jnp.where(lower, 0.0, taps_at).astype(BF16)
        rate, _, _ = modes(b)
        coef_e[b] = jnp.exp(-rate * (ROWS - 1.0 - iota(0).astype(F32))).astype(BF16)
        return carried

    def build_forward(b, carried):
        rate, weights, weight = modes(b)
        row_at = iota(0).astype(F32)
        lag = jnp.where(iota(0) == 0, 0.0, ROWS - row_at)
        carry[b] = weight * jnp.exp(-rate * (row_at + 1.0))
        per_mode = jnp.where(iota(1, (ORDER, LANES)) % ORDER == iota(0, (ORDER, LANES)), rate, 0.0)
        to_channels = (iota(0) // ORDER == iota(1) // GROUP).astype(F32)
        decay[b] = jnp.exp(-ROWS * dot(per_mode, to_channels, precision=HIGHEST))
        behind = dot(weights, jnp.exp(-rate * lag), b_dim=1, precision=HIGHEST)
        lower = iota(0) >= iota(1)
        for g in range(8):
            tf[b, pl.ds(g * ROWS, ROWS), :] = jnp.where(lower, skew(behind[g : g + 1]), 0.0).astype(BF16)
        return carried

    def build_back(b, carried):
        rate, weights, weight = modes(b)
        row_at = iota(0).astype(F32)
        falling = jnp.exp(-rate * row_at)
        coef_a[b] = falling.astype(BF16)
        back[b] = weight * jnp.exp(-rate * (ROWS - row_at))
        ahead = dot(weights, falling, b_dim=1, precision=HIGHEST)
        upper = iota(1) >= iota(0)
        for g in range(8):
            tb[b, pl.ds(g * ROWS, ROWS), :] = jnp.where(upper, skew(ahead[g : g + 1]), 0.0).astype(BF16)
        return carried

    def each(half, function):
        lax.fori_loop(half * HALF_BLOCKS, (half + 1) * HALF_BLOCKS, function, 0)

    def convolve(b, carried):
        lanes = lanes_of(b)
        before = jnp.where(c > 0, halo[:, lanes], jnp.zeros((ROWS, LANES), BF16))
        both = jnp.concatenate([prod[:, lanes], before], axis=0)
        out = own_groups(dot(mr[b], both))
        conv[:, lanes] = out
        mix = (q_ref[:, lanes].astype(F32) * out).astype(BF16)
        mixed[:, lanes] = mix
        ends[:, lanes] = fold_modes(dot(coef_e[b], mix, a_dim=0)).astype(BF16)
        return carried

    def state_copy(half, s):
        lanes = halves[half]
        return remote(
            ends.at[:, lanes], ends_all.at[c, :, lanes], st_send.at[0, half, s], st_recv.at[0, half, c], ctx=ctx(s)
        )

    def state_in(half, source):
        lanes = halves[half]
        return remote(
            ends.at[:, lanes], ends_all.at[source, :, lanes], st_send.at[0, half, 0], st_recv.at[0, half, source],
            ctx=source,
        )

    def back_copy(half, s):
        lanes = halves[half]
        return remote(
            starts.at[:, lanes], starts_all.at[c, :, lanes], st_send.at[1, half, s], st_recv.at[1, half, c],
            ctx=ctx(-s),
        )

    def back_in(half, source):
        lanes = halves[half]
        return remote(
            starts.at[:, lanes], starts_all.at[source, :, lanes], st_send.at[1, half, 0],
            st_recv.at[1, half, source], ctx=source,
        )

    def gather_states(half, incoming, received, order, wanted):
        state[:, halves[half]] = jnp.zeros((ORDER, HALF), F32)
        for source in order:
            @pl.when(wanted(source))
            def _():
                incoming(half, source).wait_recv()
                for b in range(half * HALF_BLOCKS, (half + 1) * HALF_BLOCKS):
                    lanes = pl.ds(b * LANES, LANES)
                    state[:, lanes] = state[:, lanes] * decay[b] + received[source, :, lanes].astype(F32)

    def local_long(b, carried):
        lanes = lanes_of(b)
        long_out[:, lanes] = own_groups(dot(tf[b], mixed[:, lanes]))
        return carried

    def finish_long(b, carried):
        lanes = lanes_of(b)
        total = long_out[:, lanes] + modal(carry[b], state[:, lanes])
        long_out[:, lanes] = total
        gall[c, :, lanes] = (g_ref[:, lanes].astype(F32) * total).astype(BF16)
        return carried

    def rows_of(sub):
        return pl.ds(sub * 64, 64)

    def ag_copy(half, way, step, sub, ahead=0):
        block = gall.at[ctx(-steps[way] * (step + ahead)), rows_of(sub), halves[half]]
        return remote(
            block, block, ag_send.at[half, way, step, sub], ag_recv.at[half, way, step, sub], ctx=ctx(steps[way])
        )

    def gather(half, step):
        for sub in range(2):
            for way in range(2):
                if step > 0 and (step < 4 or sub == way):
                    ag_copy(half, way, step - 1, sub, 1).wait_recv()
                if step < 3 or (step == 3 and sub == way):
                    ag_copy(half, way, step, sub).start()

    def rs_copy(half, way, step, sub):
        rows = rows_of(sub)
        return remote(
            rs_out.at[half, way, step, rows, :], rs_in.at[half, way, step, rows, :],
            rs_send.at[half, way, step, sub], rs_recv.at[half, way, step, sub], ctx=ctx(steps[way]),
        )

    def reduce(half, step):
        lanes = halves[half]
        for sub in range(2):
            rows = rows_of(sub)
            for way in range(2):
                arrives = step > 1 or (step == 1 and sub == way)
                if arrives:
                    rs_copy(half, way, step - 1, sub).wait_recv()
                if step == 4 or (step == 0 and sub != way):
                    continue
                total = part[ctx(steps[way] * (4 - step)), rows, lanes]
                if arrives:
                    total = total + rs_in[half, way, step - 1, rows, :].astype(F32)
                rs_out[half, way, step, rows, :] = total.astype(BF16)
                rs_copy(half, way, step, sub).start()

    def project(n, carried):
        channels = pl.ds(pl.multiple_of(n * FEATS, FEATS), FEATS)
        total = jnp.zeros((N_CTX * ROWS, FEATS), F32)
        rows = og[...].reshape(N_CTX * ROWS, WIDTH)
        for j in range(N_DP):
            total = total + dot(rows[:, j * FEATS : (j + 1) * FEATS], wg[j, channels, :], b_dim=1)
        part[:, :, channels] = total.reshape(N_CTX, ROWS, FEATS)
        return carried

    def project_half(half):
        for s in range(1, N_DP):
            w_in(half, s).wait_recv()
        lax.fori_loop(half * 2, half * 2 + 2, project, 0)

    def begin_back_of(half):
        def begin_back(b, carried):
            lanes = lanes_of(b)
            inner = pl.ds(pl.multiple_of((b - half * HALF_BLOCKS) * LANES, LANES), LANES)
            total = (
                part[c, :, lanes]
                + rs_in[half, 0, 3, :, inner].astype(F32)
                + rs_in[half, 1, 3, :, inner].astype(F32)
            )
            delta[:, lanes] = total
            gg_ref[:, lanes] = (total * long_out[:, lanes]).astype(BF16)
            seed = (total * g_ref[:, lanes].astype(F32)).astype(BF16)
            starts[:, lanes] = fold_modes(dot(coef_a[b], seed, a_dim=0)).astype(BF16)
            return carried

        each(half, begin_back)
        for s in range(1, N_CTX):
            @pl.when(c - s >= 0)
            def _():
                back_copy(half, s).start()

    def local_back(b, carried):
        lanes = lanes_of(b)
        seed = (delta[:, lanes] * g_ref[:, lanes].astype(F32)).astype(BF16)
        delta[:, lanes] = own_groups(dot(tb[b], seed))
        return carried

    def finish_back(b, carried):
        lanes = lanes_of(b)
        total = delta[:, lanes] + modal(back[b], state[:, lanes])
        qg_ref[:, lanes] = (total * conv[:, lanes]).astype(BF16)
        cg_ref[:, lanes] = (total * q_ref[:, lanes].astype(F32)).astype(BF16)
        return carried

    def weight_part(half, owner):
        rows = pl.ds(pl.multiple_of(owner * FEATS, FEATS), FEATS)
        return dot(ogt[rows, :], gall[:, :, halves[half]].reshape(N_CTX * ROWS, HALF))

    def x_far_copy(half, way):
        return remote(
            x_far_out.at[half, way], x_far_in.at[half, way],
            x_send.at[half, way], x_recv.at[half, way], dp=dp(steps[way]),
        )

    def x_near_copy(half, way):
        return remote(
            x_near_out.at[half, way], x_near_in.at[half, way],
            x_send.at[half, 2 + way], x_recv.at[half, 2 + way], dp=dp(steps[way]),
        )

    def weight_far(half):
        opposite = weight_part(half, dp(2))
        for way in range(2):
            x_far_out[half, way] = opposite[way * 128 : (way + 1) * 128].astype(BF16)
            x_far_copy(half, way).start()

    def weight_near(half):
        for way in range(2):
            near = weight_part(half, dp(steps[way]))
            mine = slice(way * 128, way * 128 + 128)
            other = slice((1 - way) * 128, (1 - way) * 128 + 128)
            x_near_out[half, way, other, :] = near[other].astype(BF16)
            x_far_copy(half, way).wait_recv()
            x_near_out[half, way, mine, :] = (near[mine] + x_far_in[half, way].astype(F32)).astype(BF16)
            x_near_copy(half, way).start()

    def weight_own(half):
        wt_sum[half] = weight_part(half, d)

    def weight_finish(half):
        own = wt_sum[half]
        for way in range(2):
            x_near_copy(half, way).wait_recv()
            own = own + x_near_in[half, way].astype(F32)
        wt_ref[:, half * HALF : (half + 1) * HALF] = own.astype(BF16)

    def strips(owner):
        return og.at[:, strip(owner), :]

    def y_copy(owner, s):
        return remote(strips(owner), strips(owner), y_send.at[s], y_recv.at[s], tp=tp(s, core))

    def sib_copy(owner, at):
        return remote(strips(owner), strips(owner), sib_send.at[at], sib_recv.at[at], tp=sibling)

    def begin_forward(half):
        halo_copy(half).wait_recv()
        each(half, convolve)
        for s in range(1, N_CTX):
            @pl.when(c + s < N_CTX)
            def _():
                state_copy(half, s).start()

    def forward(half):
        each(half, local_long)
        gather_states(half, state_in, ends_all, range(N_CTX - 1), lambda source: source < c)
        each(half, finish_long)
        gather(half, 0)

    def begin_y():
        for j in range(N_DP):
            feature_own(j).wait()
            for s in range(1, N_CTX):
                feature_wait(j, s)
        for s in (2, 1, 3):
            y_copy(t, s).start()
        sib_copy(t, 0).start()

    def forward_y():
        for s in range(1, N_Y):
            owner = tp(-s, core)
            y_copy(owner, s).wait_recv()
            sib_copy(owner, s).start()

    def transpose_rows(at, carried):
        ogt[:, pl.ds(pl.multiple_of(at * ROWS, ROWS), ROWS)] = og[at].T
        return carried

    each(0, build_mr)
    begin_forward(0)
    each(1, build_mr)
    each(0, build_forward)
    begin_y()
    begin_forward(1)
    forward(0)
    each(1, build_forward)
    forward(1)
    gather(0, 1)
    gather(1, 1)
    forward_y()
    each(0, build_back)
    gather(0, 2)
    each(1, build_back)
    gather(1, 2)
    w_own.wait()
    for s in range(N_Y):
        sib_copy(tp(-s, 1 - core), s).wait_recv()
    project_half(0)
    reduce(0, 0)
    gather(0, 3)
    project_half(1)
    reduce(1, 0)
    gather(1, 3)
    reduce(0, 1)
    lax.fori_loop(0, N_CTX, transpose_rows, 0)
    reduce(1, 1)
    gather(0, 4)
    weight_far(0)
    reduce(0, 2)
    gather(1, 4)
    reduce(1, 2)
    weight_far(1)
    weight_near(0)
    reduce(0, 3)
    reduce(1, 3)
    reduce(0, 4)
    begin_back_of(0)
    weight_near(1)
    each(0, local_back)
    reduce(1, 4)
    begin_back_of(1)
    each(1, local_back)
    gather_states(0, back_in, starts_all, range(N_CTX - 1, 0, -1), lambda source: source > c)
    each(0, finish_back)
    weight_own(0)
    weight_own(1)
    weight_finish(0)
    gather_states(1, back_in, starts_all, range(N_CTX - 1, 0, -1), lambda source: source > c)
    each(1, finish_back)
    weight_finish(1)

    for s in range(1, N_CTX):
        for j in range(N_DP):
            feature_copy(j, s).wait_send()

        @pl.when(c + s < N_CTX)
        def _():
            for half in range(2):
                state_copy(half, s).wait_send()

        @pl.when(c - s >= 0)
        def _():
            for half in range(2):
                back_copy(half, s).wait_send()
    for s in range(1, N_Y):
        y_copy(t, s).wait_send()
    for s in range(N_Y):
        sib_copy(tp(-s, core), s).wait_send()
    for half in range(2):
        halo_copy(half).wait_send()
        for s in range(1, N_DP):
            w_copy(half, s).wait_send()
        for way in range(2):
            x_far_copy(half, way).wait_send()
            x_near_copy(half, way).wait_send()
            for step in range(4):
                for sub in range(2):
                    if step > 0 or sub == way:
                        rs_copy(half, way, step, sub).wait_send()
                    if step < 3 or sub == way:
                        ag_copy(half, way, step, sub).wait_send()


def on_device(query, key_in, value_in, gate, out_grad, proj_weight, mr_filter, lr_rate, lr_residue):
    vmem = pl.BlockSpec(memory_space=pltpu.VMEM)
    hbm = pl.BlockSpec(memory_space=pl.ANY)
    act = jax.ShapeDtypeStruct((ROWS, WIDTH), BF16)
    outs = (act, act, act, jax.ShapeDtypeStruct((FEATS, WIDTH), BF16))
    dma = pltpu.SemaphoreType.DMA
    stacked = (BLOCKS, 8 * ROWS, LANES)
    return pl.pallas_call(
        kernel,
        out_shape=tuple(pltpu.VMEM(out.shape, out.dtype) for out in outs),
        in_specs=[vmem, vmem, vmem, vmem, hbm, hbm, vmem, vmem, vmem],
        out_specs=(vmem, vmem, vmem, vmem),
        scratch_shapes=[
            pltpu.VMEM((ROWS, WIDTH), BF16),
            pltpu.VMEM((ROWS, WIDTH), BF16),
            pltpu.VMEM((N_CTX, ROWS, WIDTH), BF16),
            pltpu.VMEM((N_DP, WIDTH, FEATS), BF16),
            pltpu.VMEM((BLOCKS, 8 * ROWS, 2 * LANES), BF16),
            pltpu.VMEM(stacked, BF16),
            pltpu.VMEM(stacked, BF16),
            pltpu.VMEM((WIDTH // GROUP, LANES), F32),
            pltpu.VMEM((WIDTH // GROUP, LANES), F32),
            pltpu.VMEM((WIDTH // GROUP, LANES), F32),
            pltpu.VMEM((BLOCKS, ROWS, LANES), BF16),
            pltpu.VMEM((BLOCKS, ROWS, LANES), BF16),
            pltpu.VMEM((BLOCKS, ROWS, LANES), F32),
            pltpu.VMEM((BLOCKS, ROWS, LANES), F32),
            pltpu.VMEM((BLOCKS, ORDER, LANES), F32),
            pltpu.VMEM((ROWS, WIDTH), F32),
            pltpu.VMEM((ROWS, WIDTH), BF16),
            pltpu.VMEM((ROWS, WIDTH), F32),
            pltpu.VMEM((N_CTX, ROWS, WIDTH), F32),
            pltpu.VMEM((ORDER, WIDTH), BF16),
            pltpu.VMEM((N_CTX, ORDER, WIDTH), BF16),
            pltpu.VMEM((ORDER, WIDTH), BF16),
            pltpu.VMEM((N_CTX, ORDER, WIDTH), BF16),
            pltpu.VMEM((ORDER, WIDTH), F32),
            pltpu.VMEM((2, 2, 4, ROWS, HALF), BF16),
            pltpu.VMEM((2, 2, 4, ROWS, HALF), BF16),
            pltpu.VMEM((N_CTX, ROWS, WIDTH), BF16),
            pltpu.VMEM((ROWS, WIDTH), F32),
            pltpu.VMEM((WIDTH, N_CTX * ROWS), BF16),
            pltpu.VMEM((2, 2, 128, HALF), BF16),
            pltpu.VMEM((2, 2, 128, HALF), BF16),
            pltpu.VMEM((2, 2, FEATS, HALF), BF16),
            pltpu.VMEM((2, 2, FEATS, HALF), BF16),
            pltpu.VMEM((2, FEATS, HALF), F32),
            dma((N_CTX, N_DP)), dma((N_CTX, N_DP)), dma((N_DP + 1,)), dma((2,)), dma((2,)),
            dma((2, N_DP)), dma((2, N_DP)), dma((N_Y,)), dma((N_Y,)), dma((N_Y,)), dma((N_Y,)),
            dma((2, 2, N_CTX)), dma((2, 2, N_CTX)), dma((2, 2, 4, 2)), dma((2, 2, 4, 2)),
            dma((2, 2, 4, 2)), dma((2, 2, 4, 2)), dma((2, N_DP)), dma((2, N_DP)),
        ],
        compiler_params=pltpu.CompilerParams(
            collective_id=0, has_side_effects=True, vmem_limit_bytes=56 * 1024 * 1024
        ),
        name="hyena_backward",
    )(query, key_in, value_in, gate, out_grad, proj_weight, mr_filter, lr_rate.T, lr_residue.T)


def solution(mesh):
    rows = P(("dp", "ctx"), "tp")
    return jax.shard_map(
        on_device,
        mesh=mesh,
        in_specs=(
            rows, rows, rows, rows, P(("dp", "ctx"), None), P("tp", ("dp", "ctx")),
            P("tp", None), P("tp", None), P("tp", None),
        ),
        out_specs=(rows, rows, rows, rows),
        check_vma=False,
    )
```
